512 devices in a mesh: grp: 32 (over y, x, core), tp: 16 (over z).
Axes of the slice: x: 4, y: 4, z: 16, core: 2. Of those that a mesh axis runs over, the one named last changes fastest.
Arguments:
- trainer_increment: float32 [1024, 128, 128], P(('tp', 'grp')), may hold values from -0.3125 to 0.3125
- trainer_residual: float32 [1024, 128, 128], P(('tp', 'grp')), may hold values from -0.3125 to 0.3125
- partition_tile_indices: int32 [512, 2], P(('tp', 'grp')), may hold values from 0 to 1, as said below
- retained_tallies: int32 [512], P(('tp', 'grp')), may hold values from 0 to 2, as said below
- projection_parameters: bfloat16 [8192, 2048], P('tp'), may hold values from -0.0625 to 0.0625
- normalized_activations: bfloat16 [4, 32, 8192], P(None, 'grp', 'tp'), may hold values from -6 to 6
- rotated_questions: bfloat16 [4, 32, 8192], P(None, 'grp'), may hold values from -256 to 256
- stored_attention_memory: bfloat16 [32, 8192, 2048], P('grp', 'tp'), may hold values from -6 to 6
- memory_fill_lengths: int32 [32], P('grp'), may hold values from 2 to 8192, as said below
Outputs:
- new_error: float32 [1024, 128, 128], P(('tp', 'grp'))
- new_kv: bfloat16 [4, 32, 2048], P(None, 'grp', 'tp')
- attention: bfloat16 [4, 32, 8192], P(None, 'grp', 'tp')
The draws below stay inside these ranges and needn't reach their ends.
Inputs may be any that keep to these rules, and one draw needn't show every extreme that they name: `partition_tile_indices`: each row lists the local block numbers of one shard, each once; only its first retained_tallies entries name surviving blocks. `retained_tallies`: some shard lists all 2 of its blocks in every draw. Row r's valid cache positions are 0 to memory_fill_lengths[r] - 1; some row has all 8192 in every draw.
All inputs are finite; a program needn't handle non-finite values.
Results may differ from the reference program's by a relative error of at most 0.02.
Values may be sent and summed in bfloat16 or wider, within the bound.
A program may use at most 64 MiB of HBM per device.

```python
import math
import jax
import jax.numpy as jnp
from jax import lax

D = 8192
HQ = 64
KVH = 8
HD = 128
BLK = 128
STEPS = 4
KVW = 2048
ROWS = 32
CACHE_LEN = 8192
CHANGE_TILES = 1024
OWNERS = 512
BPD = 2


def shared_attention(key):
    cache = jax.random.normal(jax.random.fold_in(key, 11), (ROWS, CACHE_LEN, KVH, 2, HD), jnp.float32)
    cache = jnp.clip(cache, -6.0, 6.0)
    query = jax.random.normal(jax.random.fold_in(key, 12), (STEPS, ROWS, KVH, HQ // KVH, HD), jnp.float32)
    query = jnp.clip(query, -6.0, 6.0)
    enlarged = jax.random.bernoulli(jax.random.fold_in(key, 15), 0.25, (1, ROWS, KVH, HQ // KVH, 1))
    factor = jax.random.uniform(jax.random.fold_in(key, 16), (1, ROWS, KVH, HQ // KVH, 1), jnp.float32, 20.0, 32.0)
    query = query * jnp.where(enlarged, factor, 1.0)
    return (cache.reshape(ROWS, CACHE_LEN, 2 * KVH * HD), query.reshape(STEPS, ROWS, HQ * HD))


def draw_stored_attention_memory(key, part):
    return shared_attention(key)[0].astype(jnp.bfloat16)


def draw_rotated_questions(key, part):
    return shared_attention(key)[1].astype(jnp.bfloat16)


def draw_memory_fill_lengths(key, part):
    lengths = jax.random.randint(jax.random.fold_in(key, 21), (ROWS,), 2, CACHE_LEN + 1)
    longest = jax.random.randint(jax.random.fold_in(key, 22), (), 0, ROWS)
    return jnp.where(jnp.arange(ROWS) == longest, CACHE_LEN, lengths).astype(jnp.int32)


def draw_partition_tile_indices(key, part):
    keys = jax.random.split(jax.random.fold_in(key, 31), OWNERS)

    def one_list(row_key):
        return jax.random.permutation(row_key, BPD)
    return jax.vmap(one_list)(keys).astype(jnp.int32)


def draw_retained_tallies(key, part):
    counts = jax.random.randint(jax.random.fold_in(key, 41), (OWNERS,), 0, BPD + 1)
    fullest = jax.random.randint(jax.random.fold_in(key, 42), (), 0, OWNERS)
    return jnp.where(jnp.arange(OWNERS) == fullest, BPD, counts).astype(jnp.int32)


def steps_of(key, shape, cuts, low, largest):
    gain, own = 1.0, jax.random.fold_in(key, 6)
    for dim, blocks in cuts:
        heights = jnp.exp(jax.random.uniform(jax.random.fold_in(own, dim), (blocks,), jnp.float32, low / len(cuts), largest / len(cuts)))
        gain = gain * jnp.repeat(heights, shape[dim] // blocks).reshape([-1 if axis == dim else 1 for axis in range(len(shape))])
    return gain


def noise(key, dims, deviation, bound, cuts=(), kind=jnp.bfloat16):
    gain = steps_of(key, dims, cuts, -0.22, 0.18) if cuts else 1.0
    entries = jax.random.normal(key, dims, jnp.float32) * deviation * gain
    return jnp.minimum(jnp.maximum(entries, -bound), bound).astype(kind)


def setup_inputs(seed: int = 0) -> dict:
    key_of = jax.random.split(jax.random.key(seed), 10)
    return {
        "trainer_increment": noise(key_of[0], (CHANGE_TILES, BLK, BLK), 0.02, 0.3125, ((0, 512),), jnp.float32),
        "trainer_residual": noise(key_of[1], (CHANGE_TILES, BLK, BLK), 0.02, 0.3125, ((0, 512),), jnp.float32),
        "partition_tile_indices": draw_partition_tile_indices(jax.random.fold_in(key_of[9], 71), 0),
        "retained_tallies": draw_retained_tallies(jax.random.fold_in(key_of[9], 71), 0),
        "projection_parameters": noise(key_of[4], (D, KVW), D ** -0.5, 0.0625, ((0, 16),)),
        "normalized_activations": noise(key_of[5], (STEPS, ROWS, D), 1.0, 6.0, ((1, 32), (2, 16))),
        "rotated_questions": draw_rotated_questions(jax.random.fold_in(key_of[9], 71), 0),
        "stored_attention_memory": draw_stored_attention_memory(jax.random.fold_in(key_of[9], 71), 0),
        "memory_fill_lengths": draw_memory_fill_lengths(jax.random.fold_in(key_of[9], 71), 0),
    }


def retained_tiles(partition_tile_indices, retained_tallies):
    slots = partition_tile_indices.shape[1]
    sorting_permutation = jnp.arange(slots, dtype=jnp.int32)
    enumerated_tiles = sorting_permutation[None, :] < retained_tallies[:, None]
    hits = (partition_tile_indices[:, :, None] == sorting_permutation[None, None, :]) & enumerated_tiles[:, :, None]
    return jnp.any(hits, axis=1)

def reference(trainer_increment, trainer_residual, partition_tile_indices, retained_tallies, projection_parameters, normalized_activations, rotated_questions, stored_attention_memory, memory_fill_lengths):
    summed = trainer_increment + trainer_residual
    retain_markers = retained_tiles(partition_tile_indices, retained_tallies).reshape(CHANGE_TILES)
    sent = jnp.where(retain_markers[:, None, None], summed.astype(jnp.bfloat16), jnp.zeros((), jnp.bfloat16))
    sent_wide = sent.astype(jnp.float32)
    new_error = summed - sent_wide
    update = sent_wide.reshape(D // BLK, KVW // BLK, BLK, BLK).transpose(0, 2, 1, 3).reshape(D, KVW)
    patched = (projection_parameters.astype(jnp.float32) + update).astype(jnp.bfloat16)
    new_kv = jnp.dot(normalized_activations.reshape(STEPS * ROWS, D), patched, preferred_element_type=jnp.float32)
    new_kv = new_kv.astype(jnp.bfloat16).reshape(STEPS, ROWS, KVW)
    group = HQ // KVH
    scale = 1.0 / math.sqrt(HD)
    cache_heads = jnp.moveaxis(stored_attention_memory.reshape(ROWS, CACHE_LEN, KVH, 2, HD), 2, 0)
    fresh_heads = jnp.moveaxis(new_kv.reshape(STEPS, ROWS, KVH, 2, HD), 2, 0)
    query_heads = jnp.moveaxis(rotated_questions.reshape(STEPS, ROWS, KVH, group, HD), 2, 0)
    position = jnp.arange(CACHE_LEN, dtype=jnp.int32)
    valid = (position[None, :] < memory_fill_lengths[:, None])[None, :, None, :]
    step_ids = jnp.arange(STEPS, dtype=jnp.int32)
    causal = (step_ids[None, :] <= step_ids[:, None])[:, None, None, :]
    highest = lax.Precision.HIGHEST

    def one_head(pieces):
        query, cache_rows_held, fresh = pieces
        query = query.astype(jnp.float32)
        cache_rows_held = cache_rows_held.astype(jnp.float32)
        fresh = fresh.astype(jnp.float32)
        older = jnp.einsum('srgd,rpd->srgp', query, cache_rows_held[:, :, 0], precision=highest) * scale
        newer = jnp.einsum('srgd,urd->srgu', query, fresh[:, :, 0], precision=highest) * scale
        older = jnp.where(valid, older, -jnp.inf)
        newer = jnp.where(causal, newer, -jnp.inf)
        probs = jax.nn.softmax(jnp.concatenate([older, newer], axis=-1), axis=-1)
        mixed = jnp.einsum('srgp,rpd->srgd', probs[..., :CACHE_LEN], cache_rows_held[:, :, 1], precision=highest)
        mixed = mixed + jnp.einsum('srgu,urd->srgd', probs[..., CACHE_LEN:], fresh[:, :, 1], precision=highest)
        return mixed
    outs = lax.map(one_head, (query_heads, cache_heads, fresh_heads))
    attention = jnp.moveaxis(outs, 0, 2).reshape(STEPS, ROWS, HQ * HD).astype(jnp.bfloat16)
    return (new_error, new_kv, attention)
```

```python
import functools
import math

import jax
import jax.numpy as jnp
from jax import lax
from jax.experimental import pallas as pl
from jax.experimental.pallas import tpu as pltpu
from jax.sharding import PartitionSpec as P

HD = 128
BLK = 128
NEG = -1e30
F32 = jnp.float32
BF16 = jnp.bfloat16
MESH = pl.DeviceIdType.MESH


def remote(src, dst, send, recv, device):
    return pltpu.make_async_remote_copy(
        src_ref=src, dst_ref=dst, send_sem=send, recv_sem=recv, device_id=device, device_id_type=MESH
    )


def kernel(
    dims,
    idx_ref,
    tally_ref,
    fill_ref,
    inc_ref,
    res_ref,
    proj_ref,
    x_ref,
    q_ref,
    cache_ref,
    err_ref,
    kv_ref,
    attn_ref,
    inc_v,
    res_v,
    proj_v,
    q_v,
    cache_v,
    qf,
    wbuf,
    xbuf,
    xf,
    zsend,
    zrecv,
    kvr,
    msend,
    mrecv,
    ssend,
    srecv,
    sf,
    err_v,
    in_sem,
    cache_sem,
    err_sem,
    w_send,
    w_recv,
    x_send,
    x_recv,
    z_send,
    z_recv,
    k_send,
    k_recv,
    m_send,
    m_recv,
    s_send,
    s_recv,
):
    ny, nx, nt, steps = dims
    g = lax.axis_index("grp")
    t = lax.axis_index("tp")
    y, h = g // nx, g % nx
    span = cache_ref.shape[0]
    group = q_ref.shape[1] // HD // nx
    scale = 1.0 / math.sqrt(HD)

    barrier = pltpu.get_barrier_semaphore()
    for k in range(1, nt):
        pl.semaphore_signal(barrier, inc=1, device_id=(g, (t + k) % nt), device_id_type=MESH)
    for k in range(1, nx):
        pl.semaphore_signal(barrier, inc=1, device_id=(y * nx + (h + k) % nx, t), device_id_type=MESH)
    for k in range(1, ny):
        pl.semaphore_signal(barrier, inc=1, device_id=(((y + k) % ny) * nx + h, t), device_id_type=MESH)

    loads = [
        pltpu.make_async_copy(inc_ref, inc_v, in_sem.at[0]),
        pltpu.make_async_copy(res_ref, res_v, in_sem.at[1]),
        pltpu.make_async_copy(
            proj_ref.at[pl.ds(pl.multiple_of(y * BLK, BLK), BLK), pl.ds(pl.multiple_of(h * 2 * HD, 2 * HD), 2 * HD)],
            proj_v,
            in_sem.at[2],
        ),
        pltpu.make_async_copy(x_ref, xbuf.at[h], in_sem.at[3]),
        pltpu.make_async_copy(q_ref, q_v, in_sem.at[4]),
    ]
    for copy in loads:
        copy.start()
    cache_loads = []
    for n in range(nx):
        cols = slice(n * 2 * HD, (n + 1) * 2 * HD)
        copy = pltpu.make_async_copy(cache_ref.at[:, cols], cache_v.at[:, cols], cache_sem.at[n])
        copy.start()
        cache_loads.append(copy)

    first, second, count = idx_ref[0, 0], idx_ref[0, 1], tally_ref[0]
    for copy in loads[:3]:
        copy.wait()
    rows = pl.ds(pl.multiple_of(y * BLK, BLK), BLK)
    for j in range(2):
        keep = ((count > 0) & (first == j)) | ((count > 1) & (second == j))
        summed = inc_v[j] + res_v[j]
        sent = jnp.where(keep, summed.astype(BF16).astype(F32), 0.0)
        err_v[j] = summed - sent
        cols = slice(j * BLK, (j + 1) * BLK)
        wbuf[rows, cols] = (proj_v[:, cols].astype(F32) + sent).astype(BF16)
    err_copy = pltpu.make_async_copy(err_v, err_ref, err_sem)
    err_copy.start()

    loads[4].wait()
    for n in range(nx * group):
        qf[n * steps : (n + 1) * steps, :] = q_v[:, n * HD : (n + 1) * HD].astype(F32)

    half = group * steps // 2
    position = t * span + lax.broadcasted_iota(jnp.int32, (1, span), 1)
    valid = position < fill_ref[0]
    lane = lax.broadcasted_iota(jnp.int32, (2 * half, HD), 1)
    stats = jnp.zeros((2 * half, HD), F32)
    for n in range(nx):
        cache_loads[n].wait()
        query = qf[n * 2 * half : (n + 1) * 2 * half, :].astype(BF16)
        keys = cache_v[:, n * 2 * HD : n * 2 * HD + HD]
        values = cache_v[:, n * 2 * HD + HD : (n + 1) * 2 * HD]
        scores = lax.dot_general(query, keys, (((1,), (1,)), ((), ())), preferred_element_type=F32) * scale
        scores = jnp.where(valid, scores, NEG)
        top = jnp.max(scores, axis=1, keepdims=True)
        probs = jnp.where(valid, jnp.exp(scores - top), 0.0)
        total = jnp.sum(probs, axis=1, keepdims=True)
        mixed = jnp.dot(probs.astype(BF16), values, preferred_element_type=F32).astype(BF16)
        for i in range(2):
            part = slice(i * half, (i + 1) * half)
            msend[2 * n + i] = mixed[part]
            column = jnp.concatenate([top[part], total[part]], axis=0)
            stats = jnp.where(lane == 2 * n + i, column, stats)
    square = jnp.concatenate([stats, jnp.zeros((HD - 2 * half, HD), F32)], axis=0)
    flipped = square.T
    for n in range(nt):
        ssend[n] = flipped[n : n + 1, :]
    mrecv[t] = msend[t]
    srecv[t] = ssend[t]

    loads[3].wait()
    pl.semaphore_wait(barrier, nt + nx + ny - 3)

    w_copies = []
    for k in range(1, ny):
        copy = remote(
            wbuf.at[rows], wbuf.at[rows], w_send.at[k], w_recv.at[y], (((y + k) % ny) * nx + h, t)
        )
        copy.start()
        w_copies.append(copy)
    x_copies = []
    for k in range(1, nx):
        copy = remote(xbuf.at[h], xbuf.at[h], x_send.at[k], x_recv.at[h], (y * nx + (h + k) % nx, t))
        copy.start()
        x_copies.append(copy)

    def far(i):
        return (t + nt // 2 + ((i + 1) // 2) * (1 - 2 * (i % 2))) % nt

    def send_partials(i, carry):
        d = far(i)
        remote(msend.at[d], mrecv.at[t], m_send.at[d], m_recv.at[t], (g, d)).start()
        remote(ssend.at[d], srecv.at[t], s_send.at[d], s_recv.at[t], (g, d)).start()
        return carry

    lax.fori_loop(0, nt - 1, send_partials, 0)

    for k in range(1, nx):
        o = (h + k) % nx
        remote(xbuf.at[o], xbuf.at[o], x_send.at[k], x_recv.at[o], (g, t)).wait_recv()
    for n in range(nx):
        xf[n * steps : (n + 1) * steps, :] = xbuf[n].astype(F32)
    for k in range(1, ny):
        o = (y + k) % ny
        there = pl.ds(pl.multiple_of(o * BLK, BLK), BLK)
        remote(wbuf.at[there], wbuf.at[there], w_send.at[k], w_recv.at[o], (g, t)).wait_recv()
    product = jnp.dot(xf[...].astype(BF16), wbuf[...], preferred_element_type=F32)
    for n in range(nx):
        zsend[n, :steps, :] = product[n * steps : (n + 1) * steps, :HD]
        zsend[n, steps:, :] = product[n * steps : (n + 1) * steps, HD:]
    zrecv[h] = zsend[h]

    z_copies = []
    for k in range(1, nx):
        o = (h + k) % nx
        copy = remote(zsend.at[o], zrecv.at[h], z_send.at[k], z_recv.at[h], (y * nx + o, t))
        copy.start()
        z_copies.append(copy)

    def wait_partials(i, carry):
        d = far(i)
        remote(msend.at[d], mrecv.at[d], m_send.at[d], m_recv.at[d], (g, d)).wait_recv()
        remote(ssend.at[d], srecv.at[d], s_send.at[d], s_recv.at[d], (g, d)).wait_recv()
        return carry

    for k in range(1, nx):
        o = (h + k) % nx
        remote(zsend.at[o], zrecv.at[o], z_send.at[k], z_recv.at[o], (g, t)).wait_recv()

    kvr[t] = zrecv[t // 2]

    def send_sums(i, carry):
        d = far(i)
        remote(zrecv.at[d // 2], kvr.at[t], k_send.at[d], k_recv.at[t], (g, d)).start()
        return carry

    lax.fori_loop(0, nt - 1, send_sums, 0)

    lax.fori_loop(0, nt - 1, wait_partials, 0)
    for n in range(nt):
        sf[n : n + 1, :] = srecv[n]
    s_all = sf[...]
    peak_all = jnp.max(s_all, axis=0, keepdims=True)
    weight = jnp.exp(s_all - peak_all)
    total_all = jnp.sum(weight * pltpu.roll(s_all, HD - half, 1), axis=0, keepdims=True)
    table = jnp.concatenate(
        [weight, total_all, peak_all, jnp.zeros((HD - nt - 2, HD), F32)], axis=0
    ).T[:half]
    numer = jnp.zeros((half, HD), F32)
    for n in range(nt):
        numer = numer + table[:, n : n + 1] * mrecv[n].astype(F32)
    total = table[:, nt : nt + 1]
    top = table[:, nt + 1 : nt + 2]
    query = qf[pl.ds(pl.multiple_of(t * half, half), half), :]
    step = lax.broadcasted_iota(jnp.int32, (half, 1), 0) % steps

    def wait_sums(i, carry):
        d = far(i)
        remote(kvr.at[d], kvr.at[d], k_send.at[d], k_recv.at[d], (g, d)).wait_recv()
        return carry

    lax.fori_loop(0, nt - 1, wait_sums, 0)
    fresh = kvr[0]
    for n in range(1, nt):
        fresh = fresh + kvr[n]
    rounded = fresh.astype(BF16).astype(F32)
    kv_ref[...] = jnp.where(t % 2 == 0, rounded[:steps], rounded[steps:]).astype(BF16)
    scores = []
    for u in range(steps):
        s = jnp.sum(query * rounded[u : u + 1, :], axis=1, keepdims=True) * scale
        scores.append(jnp.where(step >= u, s, NEG))
    peak = top
    for s in scores:
        peak = jnp.maximum(peak, s)
    carried = jnp.exp(top - peak)
    denom = total * carried
    numer = numer * carried
    for u in range(steps):
        p = jnp.where(step >= u, jnp.exp(scores[u] - peak), 0.0)
        denom = denom + p
        numer = numer + p * rounded[steps + u : steps + u + 1, :]
    result = numer / denom
    for n in range(half // steps):
        attn_ref[:, n * HD : (n + 1) * HD] = result[n * steps : (n + 1) * steps, :].astype(BF16)

    err_copy.wait()
    for copy in w_copies + x_copies + z_copies:
        copy.wait_send()

    def drain(i, carry):
        d = far(i)
        remote(msend.at[d], mrecv.at[d], m_send.at[d], m_recv.at[d], (g, d)).wait_send()
        remote(ssend.at[d], srecv.at[d], s_send.at[d], s_recv.at[d], (g, d)).wait_send()
        remote(kvr.at[d], kvr.at[d], k_send.at[d], k_recv.at[d], (g, d)).wait_send()
        return carry

    lax.fori_loop(0, nt - 1, drain, 0)


def body(
    trainer_increment,
    trainer_residual,
    partition_tile_indices,
    retained_tallies,
    projection_parameters,
    normalized_activations,
    rotated_questions,
    stored_attention_memory,
    memory_fill_lengths,
):
    local_feats, kvw = projection_parameters.shape
    ny = local_feats // BLK
    nx = kvw // (2 * HD)
    nt = lax.axis_size("tp")
    steps = normalized_activations.shape[0]
    span = stored_attention_memory.shape[1]
    qwidth = rotated_questions.shape[2]
    half = qwidth // HD // nx * steps // 2
    hbm = pl.BlockSpec(memory_space=pl.ANY)
    vmem = pl.BlockSpec(memory_space=pltpu.VMEM)
    smem = pl.BlockSpec(memory_space=pltpu.SMEM)
    dma = pltpu.SemaphoreType.DMA
    new_error, new_kv, attention = pl.pallas_call(
        functools.partial(kernel, (ny, nx, nt, steps)),
        out_shape=(
            jax.ShapeDtypeStruct(trainer_increment.shape, F32),
            jax.ShapeDtypeStruct((steps, kvw // nt), BF16),
            jax.ShapeDtypeStruct((steps, qwidth // nt), BF16),
        ),
        in_specs=[smem, smem, smem, hbm, hbm, hbm, hbm, hbm, hbm],
        out_specs=(hbm, vmem, vmem),
        scratch_shapes=[
            pltpu.VMEM((2, BLK, BLK), F32),
            pltpu.VMEM((2, BLK, BLK), F32),
            pltpu.VMEM((BLK, 2 * HD), BF16),
            pltpu.VMEM((steps, qwidth), BF16),
            pltpu.VMEM((span, kvw), BF16),
            pltpu.VMEM((qwidth // HD * steps, HD), F32),
            pltpu.VMEM((local_feats, 2 * HD), BF16),
            pltpu.VMEM((nx, steps, local_feats), BF16),
            pltpu.VMEM((nx * steps, local_feats), F32),
            pltpu.VMEM((nx, 2 * steps, HD), F32),
            pltpu.VMEM((nx, 2 * steps, HD), F32),
            pltpu.VMEM((nt, 2 * steps, HD), F32),
            pltpu.VMEM((nt, half, HD), BF16),
            pltpu.VMEM((nt, half, HD), BF16),
            pltpu.VMEM((nt, 1, HD), F32),
            pltpu.VMEM((nt, 1, HD), F32),
            pltpu.VMEM((nt, HD), F32),
            pltpu.VMEM((2, BLK, BLK), F32),
            dma((5,)),
            dma((nx,)),
            dma,
            dma((ny,)),
            dma((ny,)),
            dma((nx,)),
            dma((nx,)),
            dma((nx,)),
            dma((nx,)),
            dma((nt,)),
            dma((nt,)),
            dma((nt,)),
            dma((nt,)),
            dma((nt,)),
            dma((nt,)),
        ],
        compiler_params=pltpu.CompilerParams(collective_id=0, has_side_effects=True),
    )(
        partition_tile_indices,
        retained_tallies,
        memory_fill_lengths,
        trainer_increment,
        trainer_residual,
        projection_parameters,
        normalized_activations.reshape(steps, local_feats),
        rotated_questions.reshape(steps, qwidth),
        stored_attention_memory.reshape(span, kvw),
    )
    return (
        new_error,
        new_kv.reshape(steps, 1, kvw // nt),
        attention.reshape(steps, 1, qwidth // nt),
    )


def solution(mesh):
    placed = (
        P(("tp", "grp"), None, None),
        P(("tp", "grp"), None, None),
        P(("tp", "grp"), None),
        P(("tp", "grp")),
        P("tp", None),
        P(None, "grp", "tp"),
        P(None, "grp", None),
        P("grp", "tp", None),
        P("grp"),
    )
    return jax.shard_map(
        body,
        mesh=mesh,
        in_specs=placed,
        out_specs=(P(("tp", "grp"), None, None), P(None, "grp", "tp"), P(None, "grp", "tp")),
        check_vma=False,
    )
```

```python
import functools
import math

import jax
import jax.numpy as jnp
from jax import lax
from jax.experimental import pallas as pl
from jax.experimental.pallas import tpu as pltpu
from jax.sharding import PartitionSpec as P

HD = 128
BLK = 128
NEG = -1e30
F32 = jnp.float32
BF16 = jnp.bfloat16
MESH = pl.DeviceIdType.MESH


def remote(src, dst, send, recv, device):
    return pltpu.make_async_remote_copy(
        src_ref=src, dst_ref=dst, send_sem=send, recv_sem=recv, device_id=device, device_id_type=MESH
    )


def kernel(
    dims,
    idx_hbm,
    tally_hbm,
    fill_hbm,
    inc_ref,
    res_ref,
    proj_ref,
    x_ref,
    q_ref,
    cache_ref,
    err_ref,
    kv_ref,
    attn_ref,
    idx_ref,
    tally_ref,
    fill_ref,
    inc_v,
    res_v,
    proj_v,
    q_v,
    cache_v,
    qf,
    wbuf,
    xbuf,
    xf,
    zsend,
    zrecv,
    kvr,
    msend,
    mrecv,
    ssend,
    srecv,
    sf,
    in_sem,
    cache_sem,
    w_send,
    w_recv,
    x_send,
    x_recv,
    z_send,
    z_recv,
    k_send,
    k_recv,
    m_send,
    m_recv,
    s_send,
    s_recv,
):
    ny, nx, nt, steps = dims
    g = lax.axis_index("grp")
    t = lax.axis_index("tp")
    y, h = g // nx, g % nx
    span = cache_ref.shape[0]
    group = q_ref.shape[1] // HD // nx
    scale = 1.0 / math.sqrt(HD)

    barrier = pltpu.get_barrier_semaphore()
    for k in range(1, nt):
        pl.semaphore_signal(barrier, inc=1, device_id=(g, (t + k) % nt), device_id_type=MESH)
    for k in range(1, nx):
        pl.semaphore_signal(barrier, inc=1, device_id=(y * nx + (h + k) % nx, t), device_id_type=MESH)
    for k in range(1, ny):
        pl.semaphore_signal(barrier, inc=1, device_id=(((y + k) % ny) * nx + h, t), device_id_type=MESH)

    loads = [
        pltpu.make_async_copy(inc_ref, inc_v, in_sem.at[0]),
        pltpu.make_async_copy(res_ref, res_v, in_sem.at[1]),
        pltpu.make_async_copy(
            proj_ref.at[pl.ds(pl.multiple_of(y * BLK, BLK), BLK), pl.ds(pl.multiple_of(h * 2 * HD, 2 * HD), 2 * HD)],
            proj_v,
            in_sem.at[2],
        ),
        pltpu.make_async_copy(x_ref, xbuf.at[h], in_sem.at[3]),
        pltpu.make_async_copy(q_ref, q_v, in_sem.at[4]),
        pltpu.make_async_copy(idx_hbm, idx_ref, in_sem.at[5]),
        pltpu.make_async_copy(tally_hbm, tally_ref, in_sem.at[6]),
        pltpu.make_async_copy(fill_hbm, fill_ref, in_sem.at[7]),
    ]
    for copy in loads:
        copy.start()
    cache_loads = []
    for n in range(nx):
        cols = slice(n * 2 * HD, (n + 1) * 2 * HD)
        copy = pltpu.make_async_copy(cache_ref.at[:, cols], cache_v.at[:, cols], cache_sem.at[n])
        copy.start()
        cache_loads.append(copy)

    for copy in loads[:4] + loads[5:]:
        copy.wait()
    first, second, count = idx_ref[0, 0], idx_ref[0, 1], tally_ref[0]
    rows = pl.ds(pl.multiple_of(y * BLK, BLK), BLK)
    for j in range(2):
        keep = ((count > 0) & (first == j)) | ((count > 1) & (second == j))
        summed = inc_v[j] + res_v[j]
        sent = jnp.where(keep, summed.astype(BF16).astype(F32), 0.0)
        err_ref[j] = summed - sent
        cols = slice(j * BLK, (j + 1) * BLK)
        wbuf[rows, cols] = (proj_v[:, cols].astype(F32) + sent).astype(BF16)
    pl.semaphore_wait(barrier, nt + nx + ny - 3)

    w_copies = []
    for k in range(1, ny):
        copy = remote(
            wbuf.at[rows], wbuf.at[rows], w_send.at[k], w_recv.at[y], (((y + k) % ny) * nx + h, t)
        )
        copy.start()
        w_copies.append(copy)
    x_copies = []
    for k in range(1, nx):
        copy = remote(xbuf.at[h], xbuf.at[h], x_send.at[k], x_recv.at[h], (y * nx + (h + k) % nx, t))
        copy.start()
        x_copies.append(copy)

    loads[4].wait()
    for n in range(nx * group):
        qf[n * steps : (n + 1) * steps, :] = q_v[:, n * HD : (n + 1) * HD].astype(F32)

    half = group * steps // 2
    position = t * span + lax.broadcasted_iota(jnp.int32, (1, span), 1)
    valid = position < fill_ref[0]
    lane = lax.broadcasted_iota(jnp.int32, (2 * half, HD), 1)
    stats = jnp.zeros((2 * half, HD), F32)
    for n in range(nx):
        cache_loads[n].wait()
        query = qf[n * 2 * half : (n + 1) * 2 * half, :].astype(BF16)
        keys = cache_v[:, n * 2 * HD : n * 2 * HD + HD]
        values = cache_v[:, n * 2 * HD + HD : (n + 1) * 2 * HD]
        scores = lax.dot_general(query, keys, (((1,), (1,)), ((), ())), preferred_element_type=F32) * scale
        scores = jnp.where(valid, scores, NEG)
        top = jnp.max(scores, axis=1, keepdims=True)
        probs = jnp.where(valid, jnp.exp(scores - top), 0.0)
        total = jnp.sum(probs, axis=1, keepdims=True)
        mixed = jnp.dot(probs.astype(BF16), values, preferred_element_type=F32).astype(BF16)
        for i in range(2):
            part = slice(i * half, (i + 1) * half)
            msend[2 * n + i] = mixed[part]
            column = jnp.concatenate([top[part], total[part]], axis=0)
            stats = jnp.where(lane == 2 * n + i, column, stats)
    square = jnp.concatenate([stats, jnp.zeros((HD - 2 * half, HD), F32)], axis=0)
    flipped = square.T
    for n in range(nt):
        ssend[n] = flipped[n : n + 1, :]
    mrecv[t] = msend[t]
    srecv[t] = ssend[t]

    def far(i):
        return (t + nt // 2 + ((i + 1) // 2) * (1 - 2 * (i % 2))) % nt

    def send_partials(i, carry):
        d = far(i)
        remote(msend.at[d], mrecv.at[t], m_send.at[d], m_recv.at[t], (g, d)).start()
        remote(ssend.at[d], srecv.at[t], s_send.at[d], s_recv.at[t], (g, d)).start()
        return carry

    lax.fori_loop(0, nt - 1, send_partials, 0)

    for k in range(1, nx):
        o = (h + k) % nx
        remote(xbuf.at[o], xbuf.at[o], x_send.at[k], x_recv.at[o], (g, t)).wait_recv()
    for n in range(nx):
        xf[n * steps : (n + 1) * steps, :] = xbuf[n].astype(F32)
    for k in range(1, ny):
        o = (y + k) % ny
        there = pl.ds(pl.multiple_of(o * BLK, BLK), BLK)
        remote(wbuf.at[there], wbuf.at[there], w_send.at[k], w_recv.at[o], (g, t)).wait_recv()
    product = jnp.dot(xf[...].astype(BF16), wbuf[...], preferred_element_type=F32)
    for n in range(nx):
        zsend[n, :steps, :] = product[n * steps : (n + 1) * steps, :HD]
        zsend[n, steps:, :] = product[n * steps : (n + 1) * steps, HD:]
    zrecv[h] = zsend[h]

    z_copies = []
    for k in range(1, nx):
        o = (h + k) % nx
        copy = remote(zsend.at[o], zrecv.at[h], z_send.at[k], z_recv.at[h], (y * nx + o, t))
        copy.start()
        z_copies.append(copy)

    def wait_partials(i, carry):
        d = far(i)
        remote(msend.at[d], mrecv.at[d], m_send.at[d], m_recv.at[d], (g, d)).wait_recv()
        remote(ssend.at[d], srecv.at[d], s_send.at[d], s_recv.at[d], (g, d)).wait_recv()
        return carry

    for k in range(1, nx):
        o = (h + k) % nx
        remote(zsend.at[o], zrecv.at[o], z_send.at[k], z_recv.at[o], (g, t)).wait_recv()

    kvr[t] = zrecv[t // 2]

    def send_sums(i, carry):
        d = far(i)
        remote(zrecv.at[d // 2], kvr.at[t], k_send.at[d], k_recv.at[t], (g, d)).start()
        return carry

    lax.fori_loop(0, nt - 1, send_sums, 0)

    lax.fori_loop(0, nt - 1, wait_partials, 0)
    for n in range(nt):
        sf[n : n + 1, :] = srecv[n]
    s_all = sf[...]
    peak_all = jnp.max(s_all, axis=0, keepdims=True)
    weight = jnp.exp(s_all - peak_all)
    total_all = jnp.sum(weight * pltpu.roll(s_all, HD - half, 1), axis=0, keepdims=True)
    table = jnp.concatenate(
        [weight, total_all, peak_all, jnp.zeros((HD - nt - 2, HD), F32)], axis=0
    ).T[:half]
    numer = jnp.zeros((half, HD), F32)
    for n in range(nt):
        numer = numer + table[:, n : n + 1] * mrecv[n].astype(F32)
    total = table[:, nt : nt + 1]
    top = table[:, nt + 1 : nt + 2]
    query = qf[pl.ds(pl.multiple_of(t * half, half), half), :]
    step = lax.broadcasted_iota(jnp.int32, (half, 1), 0) % steps

    def wait_sums(i, carry):
        d = far(i)
        remote(kvr.at[d], kvr.at[d], k_send.at[d], k_recv.at[d], (g, d)).wait_recv()
        return carry

    lax.fori_loop(0, nt - 1, wait_sums, 0)
    fresh = kvr[0]
    for n in range(1, nt):
        fresh = fresh + kvr[n]
    rounded = fresh.astype(BF16).astype(F32)
    kv_ref[...] = jnp.where(t % 2 == 0, rounded[:steps], rounded[steps:]).astype(BF16)
    scores = []
    for u in range(steps):
        s = jnp.sum(query * rounded[u : u + 1, :], axis=1, keepdims=True) * scale
        scores.append(jnp.where(step >= u, s, NEG))
    peak = top
    for s in scores:
        peak = jnp.maximum(peak, s)
    carried = jnp.exp(top - peak)
    denom = total * carried
    numer = numer * carried
    for u in range(steps):
        p = jnp.where(step >= u, jnp.exp(scores[u] - peak), 0.0)
        denom = denom + p
        numer = numer + p * rounded[steps + u : steps + u + 1, :]
    result = numer / denom
    for n in range(half // steps):
        attn_ref[:, n * HD : (n + 1) * HD] = result[n * steps : (n + 1) * steps, :].astype(BF16)

    for copy in w_copies + x_copies + z_copies:
        copy.wait_send()

    def drain(i, carry):
        d = far(i)
        remote(msend.at[d], mrecv.at[d], m_send.at[d], m_recv.at[d], (g, d)).wait_send()
        remote(ssend.at[d], srecv.at[d], s_send.at[d], s_recv.at[d], (g, d)).wait_send()
        remote(kvr.at[d], kvr.at[d], k_send.at[d], k_recv.at[d], (g, d)).wait_send()
        return carry

    lax.fori_loop(0, nt - 1, drain, 0)


def put_out(err_ref, kv_ref, attn_ref, err_out, kv_out, attn_out, sem):
    copies = [
        pltpu.make_async_copy(err_ref, err_out, sem.at[0]),
        pltpu.make_async_copy(kv_ref, kv_out, sem.at[1]),
        pltpu.make_async_copy(attn_ref, attn_out, sem.at[2]),
    ]
    for copy in copies:
        copy.start()
    for copy in copies:
        copy.wait()


def body(
    trainer_increment,
    trainer_residual,
    partition_tile_indices,
    retained_tallies,
    projection_parameters,
    normalized_activations,
    rotated_questions,
    stored_attention_memory,
    memory_fill_lengths,
):
    local_feats, kvw = projection_parameters.shape
    ny = local_feats // BLK
    nx = kvw // (2 * HD)
    nt = lax.axis_size("tp")
    steps = normalized_activations.shape[0]
    span = stored_attention_memory.shape[1]
    qwidth = rotated_questions.shape[2]
    half = qwidth // HD // nx * steps // 2
    hbm = pl.BlockSpec(memory_space=pltpu.HBM)
    anywhere = pl.BlockSpec(memory_space=pl.ANY)
    vmem = pl.BlockSpec(memory_space=pltpu.VMEM)
    dma = pltpu.SemaphoreType.DMA
    new_error, new_kv, attention = pl.pallas_call(
        functools.partial(kernel, (ny, nx, nt, steps)),
        out_shape=(
            pltpu.VMEM(trainer_increment.shape, F32),
            pltpu.VMEM((steps, kvw // nt), BF16),
            pltpu.VMEM((steps, qwidth // nt), BF16),
        ),
        in_specs=[hbm, hbm, hbm, hbm, hbm, hbm, hbm, hbm, hbm],
        out_specs=(vmem, vmem, vmem),
        scratch_shapes=[
            pltpu.SMEM((1, 2), jnp.int32),
            pltpu.SMEM((1,), jnp.int32),
            pltpu.SMEM((1,), jnp.int32),
            pltpu.VMEM((2, BLK, BLK), F32),
            pltpu.VMEM((2, BLK, BLK), F32),
            pltpu.VMEM((BLK, 2 * HD), BF16),
            pltpu.VMEM((steps, qwidth), BF16),
            pltpu.VMEM((span, kvw), BF16),
            pltpu.VMEM((qwidth // HD * steps, HD), F32),
            pltpu.VMEM((local_feats, 2 * HD), BF16),
            pltpu.VMEM((nx, steps, local_feats), BF16),
            pltpu.VMEM((nx * steps, local_feats), F32),
            pltpu.VMEM((nx, 2 * steps, HD), F32),
            pltpu.VMEM((nx, 2 * steps, HD), F32),
            pltpu.VMEM((nt, 2 * steps, HD), F32),
            pltpu.VMEM((nt, half, HD), BF16),
            pltpu.VMEM((nt, half, HD), BF16),
            pltpu.VMEM((nt, 1, HD), F32),
            pltpu.VMEM((nt, 1, HD), F32),
            pltpu.VMEM((nt, HD), F32),
            dma((8,)),
            dma((nx,)),
            dma((ny,)),
            dma((ny,)),
            dma((nx,)),
            dma((nx,)),
            dma((nx,)),
            dma((nx,)),
            dma((nt,)),
            dma((nt,)),
            dma((nt,)),
            dma((nt,)),
            dma((nt,)),
            dma((nt,)),
        ],
        compiler_params=pltpu.CompilerParams(collective_id=0, has_side_effects=True),
    )(
        partition_tile_indices,
        retained_tallies,
        memory_fill_lengths,
        trainer_increment,
        trainer_residual,
        projection_parameters,
        normalized_activations.reshape(steps, local_feats),
        rotated_questions.reshape(steps, qwidth),
        stored_attention_memory.reshape(span, kvw),
    )
    outs = (new_error, new_kv, attention)
    new_error, new_kv, attention = pl.pallas_call(
        put_out,
        out_shape=tuple(jax.ShapeDtypeStruct(out.shape, out.dtype) for out in outs),
        in_specs=[anywhere] * 3,
        out_specs=(hbm,) * 3,
        scratch_shapes=[dma((3,))],
    )(*(pltpu.with_memory_space_constraint(out, pltpu.VMEM) for out in outs))
    return (
        new_error,
        new_kv.reshape(steps, 1, kvw // nt),
        attention.reshape(steps, 1, qwidth // nt),
    )


def solution(mesh):
    placed = (
        P(("tp", "grp"), None, None),
        P(("tp", "grp"), None, None),
        P(("tp", "grp"), None),
        P(("tp", "grp")),
        P("tp", None),
        P(None, "grp", "tp"),
        P(None, "grp", None),
        P("grp", "tp", None),
        P("grp"),
    )
    return jax.shard_map(
        body,
        mesh=mesh,
        in_specs=placed,
        out_specs=(P(("tp", "grp"), None, None), P(None, "grp", "tp"), P(None, "grp", "tp")),
        check_vma=False,
    )
```

```python
import functools
import math

import jax
import jax.numpy as jnp
from jax import lax
from jax.experimental import pallas as pl
from jax.experimental.pallas import tpu as pltpu
from jax.sharding import PartitionSpec as P

HD = 128
BLK = 128
NEG = -1e30
F32 = jnp.float32
BF16 = jnp.bfloat16
MESH = pl.DeviceIdType.MESH


def remote(src, dst, send, recv, device):
    return pltpu.make_async_remote_copy(
        src_ref=src, dst_ref=dst, send_sem=send, recv_sem=recv, device_id=device, device_id_type=MESH
    )


def kernel(
    dims,
    idx_hbm,
    tally_hbm,
    fill_hbm,
    inc_ref,
    res_ref,
    proj_ref,
    x_ref,
    q_ref,
    cache_ref,
    err_ref,
    kv_ref,
    attn_ref,
    idx_ref,
    tally_ref,
    fill_ref,
    inc_v,
    res_v,
    proj_v,
    q_v,
    cache_v,
    qf,
    wbuf,
    xbuf,
    xf,
    zsend,
    zrecv,
    kvr,
    msend,
    mrecv,
    ssend,
    srecv,
    sf,
    in_sem,
    cache_sem,
    w_send,
    w_recv,
    x_send,
    x_recv,
    z_send,
    z_recv,
    k_send,
    k_recv,
    m_send,
    m_recv,
    s_send,
    s_recv,
    known,
):
    ny, nx, nt, steps = dims
    g = lax.axis_index("grp")
    t = lax.axis_index("tp")
    y, h = g // nx, g % nx
    span = cache_ref.shape[0]
    group = q_ref.shape[1] // HD // nx
    scale = 1.0 / math.sqrt(HD)

    loads = [
        pltpu.make_async_copy(inc_ref, inc_v, in_sem.at[0]),
        pltpu.make_async_copy(res_ref, res_v, in_sem.at[1]),
        pltpu.make_async_copy(
            proj_ref.at[pl.ds(pl.multiple_of(y * BLK, BLK), BLK), pl.ds(pl.multiple_of(h * 2 * HD, 2 * HD), 2 * HD)],
            proj_v,
            in_sem.at[2],
        ),
        pltpu.make_async_copy(x_ref, xbuf.at[h], in_sem.at[3]),
        pltpu.make_async_copy(q_ref, q_v, in_sem.at[4]),
        pltpu.make_async_copy(idx_hbm, idx_ref, in_sem.at[5]),
        pltpu.make_async_copy(tally_hbm, tally_ref, in_sem.at[6]),
        pltpu.make_async_copy(fill_hbm, fill_ref, in_sem.at[7]),
    ]
    for copy in loads:
        copy.start()
    cache_loads = []
    for n in range(nx):
        cols = slice(n * 2 * HD, (n + 1) * 2 * HD)
        copy = pltpu.make_async_copy(cache_ref.at[:, cols], cache_v.at[:, cols], cache_sem.at[n])
        copy.start()
        cache_loads.append(copy)

    barrier = pltpu.get_barrier_semaphore()
    for k in (1, nt - 1):
        pl.semaphore_signal(barrier, inc=1, device_id=(g, (t + k) % nt), device_id_type=MESH)
    for k in range(1, nx):
        pl.semaphore_signal(barrier, inc=1, device_id=(y * nx + (h + k) % nx, t), device_id_type=MESH)
    for k in range(1, ny):
        pl.semaphore_signal(barrier, inc=1, device_id=(((y + k) % ny) * nx + h, t), device_id_type=MESH)

    for copy in loads[:4] + loads[5:]:
        copy.wait()
    first, second, count = idx_ref[0, 0], idx_ref[0, 1], tally_ref[0]
    rows = pl.ds(pl.multiple_of(y * BLK, BLK), BLK)
    for j in range(2):
        keep = ((count > 0) & (first == j)) | ((count > 1) & (second == j))
        summed = inc_v[j] + res_v[j]
        sent = jnp.where(keep, summed.astype(BF16).astype(F32), 0.0)
        err_ref[j] = summed - sent
        cols = slice(j * BLK, (j + 1) * BLK)
        wbuf[rows, cols] = (proj_v[:, cols].astype(F32) + sent).astype(BF16)
    pl.semaphore_wait(barrier, nx + ny)

    reach = [1 << r for r in range(8) if (1 << r) < nt // 2]

    def tell(r):
        for k in (reach[r], nt - reach[r]):
            pl.semaphore_signal(known.at[r], inc=1, device_id=(g, (t + k) % nt), device_id_type=MESH)

    def learn(r):
        if 0 <= r < len(reach):
            pl.semaphore_wait(known.at[r], 2)
            if r + 1 < len(reach):
                tell(r + 1)

    tell(0)

    w_copies = []
    for k in range(1, ny):
        copy = remote(
            wbuf.at[rows], wbuf.at[rows], w_send.at[k], w_recv.at[y], (((y + k) % ny) * nx + h, t)
        )
        copy.start()
        w_copies.append(copy)
    x_copies = []
    for k in range(1, nx):
        copy = remote(xbuf.at[h], xbuf.at[h], x_send.at[k], x_recv.at[h], (y * nx + (h + k) % nx, t))
        copy.start()
        x_copies.append(copy)

    loads[4].wait()
    for n in range(nx * group):
        qf[n * steps : (n + 1) * steps, :] = q_v[:, n * HD : (n + 1) * HD].astype(F32)

    half = group * steps // 2
    position = t * span + lax.broadcasted_iota(jnp.int32, (1, span), 1)
    valid = position < fill_ref[0]
    lane = lax.broadcasted_iota(jnp.int32, (2 * half, HD), 1)
    stats = jnp.zeros((2 * half, HD), F32)
    for n in range(nx):
        cache_loads[n].wait()
        query = qf[n * 2 * half : (n + 1) * 2 * half, :].astype(BF16)
        keys = cache_v[:, n * 2 * HD : n * 2 * HD + HD]
        values = cache_v[:, n * 2 * HD + HD : (n + 1) * 2 * HD]
        scores = lax.dot_general(query, keys, (((1,), (1,)), ((), ())), preferred_element_type=F32) * scale
        scores = jnp.where(valid, scores, NEG)
        top = jnp.max(scores, axis=1, keepdims=True)
        probs = jnp.where(valid, jnp.exp(scores - top), 0.0)
        total = jnp.sum(probs, axis=1, keepdims=True)
        mixed = jnp.dot(probs.astype(BF16), values, preferred_element_type=F32).astype(BF16)
        for i in range(2):
            part = slice(i * half, (i + 1) * half)
            msend[2 * n + i] = mixed[part]
            column = jnp.concatenate([top[part], total[part]], axis=0)
            stats = jnp.where(lane == 2 * n + i, column, stats)
        if n == nx // 2 - 1:
            learn(len(reach) - 3)
    learn(len(reach) - 2)
    square = jnp.concatenate([stats, jnp.zeros((HD - 2 * half, HD), F32)], axis=0)
    flipped = square.T
    for n in range(nt):
        ssend[n] = flipped[n : n + 1, :]
    mrecv[t] = msend[t]
    srecv[t] = ssend[t]

    def far(i):
        return (t + nt // 2 + ((i + 1) // 2) * (1 - 2 * (i % 2))) % nt

    def send_partials(i, carry):
        d = far(i)
        remote(msend.at[d], mrecv.at[t], m_send.at[d], m_recv.at[t], (g, d)).start()
        remote(ssend.at[d], srecv.at[t], s_send.at[d], s_recv.at[t], (g, d)).start()
        return carry


    for k in range(1, nx):
        o = (h + k) % nx
        remote(xbuf.at[o], xbuf.at[o], x_send.at[k], x_recv.at[o], (g, t)).wait_recv()
    for n in range(nx):
        xf[n * steps : (n + 1) * steps, :] = xbuf[n].astype(F32)
    for k in range(1, ny):
        o = (y + k) % ny
        there = pl.ds(pl.multiple_of(o * BLK, BLK), BLK)
        remote(wbuf.at[there], wbuf.at[there], w_send.at[k], w_recv.at[o], (g, t)).wait_recv()
    product = jnp.dot(xf[...].astype(BF16), wbuf[...], preferred_element_type=F32)
    for n in range(nx):
        zsend[n, :steps, :] = product[n * steps : (n + 1) * steps, :HD]
        zsend[n, steps:, :] = product[n * steps : (n + 1) * steps, HD:]
    zrecv[h] = zsend[h]

    z_copies = []
    for k in range(1, nx):
        o = (h + k) % nx
        copy = remote(zsend.at[o], zrecv.at[h], z_send.at[k], z_recv.at[h], (y * nx + o, t))
        copy.start()
        z_copies.append(copy)

    learn(len(reach) - 1)
    lax.fori_loop(0, nt - 1, send_partials, 0)

    def wait_partials(i, carry):
        d = far(i)
        remote(msend.at[d], mrecv.at[d], m_send.at[d], m_recv.at[d], (g, d)).wait_recv()
        remote(ssend.at[d], srecv.at[d], s_send.at[d], s_recv.at[d], (g, d)).wait_recv()
        return carry

    def send_sums(i, carry):
        o = (h + i) % nx

        @pl.when(i > 0)
        def _():
            remote(zsend.at[o], zrecv.at[o], z_send.at[i], z_recv.at[o], (g, t)).wait_recv()

        for j in range(2):
            d = 2 * o + j

            @pl.when(d != t)
            def _():
                remote(zrecv.at[o], kvr.at[t], k_send.at[d], k_recv.at[t], (g, d)).start()

        return carry

    lax.fori_loop(0, nx, send_sums, 0)
    kvr[t] = zrecv[t // 2]

    lax.fori_loop(0, nt - 1, wait_partials, 0)
    for n in range(nt):
        sf[n : n + 1, :] = srecv[n]
    s_all = sf[...]
    peak_all = jnp.max(s_all, axis=0, keepdims=True)
    weight = jnp.exp(s_all - peak_all)
    total_all = jnp.sum(weight * pltpu.roll(s_all, HD - half, 1), axis=0, keepdims=True)
    table = jnp.concatenate(
        [weight, total_all, peak_all, jnp.zeros((HD - nt - 2, HD), F32)], axis=0
    ).T[:half]
    numer = jnp.zeros((half, HD), F32)
    for n in range(nt):
        numer = numer + table[:, n : n + 1] * mrecv[n].astype(F32)
    total = table[:, nt : nt + 1]
    top = table[:, nt + 1 : nt + 2]
    query = qf[pl.ds(pl.multiple_of(t * half, half), half), :]
    step = lax.broadcasted_iota(jnp.int32, (half, 1), 0) % steps

    def wait_sums(i, carry):
        d = far(i)
        remote(kvr.at[d], kvr.at[d], k_send.at[d], k_recv.at[d], (g, d)).wait_recv()
        return carry

    lax.fori_loop(0, nt - 1, wait_sums, 0)
    fresh = kvr[0]
    for n in range(1, nt):
        fresh = fresh + kvr[n]
    rounded = fresh.astype(BF16).astype(F32)
    kv_ref[...] = jnp.where(t % 2 == 0, rounded[:steps], rounded[steps:]).astype(BF16)
    scores = []
    for u in range(steps):
        s = jnp.sum(query * rounded[u : u + 1, :], axis=1, keepdims=True) * scale
        scores.append(jnp.where(step >= u, s, NEG))
    peak = top
    for s in scores:
        peak = jnp.maximum(peak, s)
    carried = jnp.exp(top - peak)
    denom = total * carried
    numer = numer * carried
    for u in range(steps):
        p = jnp.where(step >= u, jnp.exp(scores[u] - peak), 0.0)
        denom = denom + p
        numer = numer + p * rounded[steps + u : steps + u + 1, :]
    result = numer / denom
    for n in range(half // steps):
        attn_ref[:, n * HD : (n + 1) * HD] = result[n * steps : (n + 1) * steps, :].astype(BF16)

    for copy in w_copies + x_copies + z_copies:
        copy.wait_send()

    def drain(i, carry):
        d = far(i)
        remote(msend.at[d], mrecv.at[d], m_send.at[d], m_recv.at[d], (g, d)).wait_send()
        remote(ssend.at[d], srecv.at[d], s_send.at[d], s_recv.at[d], (g, d)).wait_send()
        remote(kvr.at[d], kvr.at[d], k_send.at[d], k_recv.at[d], (g, d)).wait_send()
        return carry

    lax.fori_loop(0, nt - 1, drain, 0)


def put_out(err_ref, kv_ref, attn_ref, err_out, kv_out, attn_out, sem):
    copies = [
        pltpu.make_async_copy(err_ref, err_out, sem.at[0]),
        pltpu.make_async_copy(kv_ref, kv_out, sem.at[1]),
        pltpu.make_async_copy(attn_ref, attn_out, sem.at[2]),
    ]
    for copy in copies:
        copy.start()
    for copy in copies:
        copy.wait()


def body(
    trainer_increment,
    trainer_residual,
    partition_tile_indices,
    retained_tallies,
    projection_parameters,
    normalized_activations,
    rotated_questions,
    stored_attention_memory,
    memory_fill_lengths,
):
    local_feats, kvw = projection_parameters.shape
    ny = local_feats // BLK
    nx = kvw // (2 * HD)
    nt = lax.axis_size("tp")
    steps = normalized_activations.shape[0]
    span = stored_attention_memory.shape[1]
    qwidth = rotated_questions.shape[2]
    half = qwidth // HD // nx * steps // 2
    hbm = pl.BlockSpec(memory_space=pltpu.HBM)
    anywhere = pl.BlockSpec(memory_space=pl.ANY)
    vmem = pl.BlockSpec(memory_space=pltpu.VMEM)
    dma = pltpu.SemaphoreType.DMA
    new_error, new_kv, attention = pl.pallas_call(
        functools.partial(kernel, (ny, nx, nt, steps)),
        out_shape=(
            pltpu.VMEM(trainer_increment.shape, F32),
            pltpu.VMEM((steps, kvw // nt), BF16),
            pltpu.VMEM((steps, qwidth // nt), BF16),
        ),
        in_specs=[hbm, hbm, hbm, hbm, hbm, hbm, hbm, hbm, hbm],
        out_specs=(vmem, vmem, vmem),
        scratch_shapes=[
            pltpu.SMEM((1, 2), jnp.int32),
            pltpu.SMEM((1,), jnp.int32),
            pltpu.SMEM((1,), jnp.int32),
            pltpu.VMEM((2, BLK, BLK), F32),
            pltpu.VMEM((2, BLK, BLK), F32),
            pltpu.VMEM((BLK, 2 * HD), BF16),
            pltpu.VMEM((steps, qwidth), BF16),
            pltpu.VMEM((span, kvw), BF16),
            pltpu.VMEM((qwidth // HD * steps, HD), F32),
            pltpu.VMEM((local_feats, 2 * HD), BF16),
            pltpu.VMEM((nx, steps, local_feats), BF16),
            pltpu.VMEM((nx * steps, local_feats), F32),
            pltpu.VMEM((nx, 2 * steps, HD), F32),
            pltpu.VMEM((nx, 2 * steps, HD), F32),
            pltpu.VMEM((nt, 2 * steps, HD), F32),
            pltpu.VMEM((nt, half, HD), BF16),
            pltpu.VMEM((nt, half, HD), BF16),
            pltpu.VMEM((nt, 1, HD), F32),
            pltpu.VMEM((nt, 1, HD), F32),
            pltpu.VMEM((nt, HD), F32),
            dma((8,)),
            dma((nx,)),
            dma((ny,)),
            dma((ny,)),
            dma((nx,)),
            dma((nx,)),
            dma((nx,)),
            dma((nx,)),
            dma((nt,)),
            dma((nt,)),
            dma((nt,)),
            dma((nt,)),
            dma((nt,)),
            dma((nt,)),
            pltpu.SemaphoreType.REGULAR((8,)),
        ],
        compiler_params=pltpu.CompilerParams(collective_id=0, has_side_effects=True),
    )(
        partition_tile_indices,
        retained_tallies,
        memory_fill_lengths,
        trainer_increment,
        trainer_residual,
        projection_parameters,
        normalized_activations.reshape(steps, local_feats),
        rotated_questions.reshape(steps, qwidth),
        stored_attention_memory.reshape(span, kvw),
    )
    outs = (new_error, new_kv, attention)
    new_error, new_kv, attention = pl.pallas_call(
        put_out,
        out_shape=tuple(jax.ShapeDtypeStruct(out.shape, out.dtype) for out in outs),
        in_specs=[anywhere] * 3,
        out_specs=(hbm,) * 3,
        scratch_shapes=[dma((3,))],
    )(*(pltpu.with_memory_space_constraint(out, pltpu.VMEM) for out in outs))
    return (
        new_error,
        new_kv.reshape(steps, 1, kvw // nt),
        attention.reshape(steps, 1, qwidth // nt),
    )


def solution(mesh):
    placed = (
        P(("tp", "grp"), None, None),
        P(("tp", "grp"), None, None),
        P(("tp", "grp"), None),
        P(("tp", "grp")),
        P("tp", None),
        P(None, "grp", "tp"),
        P(None, "grp", None),
        P("grp", "tp", None),
        P("grp"),
    )
    return jax.shard_map(
        body,
        mesh=mesh,
        in_specs=placed,
        out_specs=(P(("tp", "grp"), None, None), P(None, "grp", "tp"), P(None, "grp", "tp")),
        check_vma=False,
    )
```

```python
import functools
import math

import jax
import jax.numpy as jnp
from jax import lax
from jax.experimental import pallas as pl
from jax.experimental.pallas import tpu as pltpu
from jax.sharding import PartitionSpec as P

HD = 128
BLK = 128
NEG = -1e30
F32 = jnp.float32
BF16 = jnp.bfloat16
MESH = pl.DeviceIdType.MESH


def remote(src, dst, send, recv, device):
    return pltpu.make_async_remote_copy(
        src_ref=src, dst_ref=dst, send_sem=send, recv_sem=recv, device_id=device, device_id_type=MESH
    )


def kernel(
    dims,
    idx_hbm,
    tally_hbm,
    fill_hbm,
    inc_ref,
    res_ref,
    proj_ref,
    x_ref,
    q_ref,
    cache_ref,
    err_ref,
    kv_ref,
    attn_ref,
    idx_ref,
    tally_ref,
    fill_ref,
    inc_v,
    res_v,
    proj_v,
    q_v,
    cache_v,
    qf,
    wbuf,
    xbuf,
    xf,
    zsend,
    zrecv,
    kvr,
    msend,
    mrecv,
    ssend,
    srecv,
    sf,
    in_sem,
    cache_sem,
    w_send,
    w_recv,
    x_send,
    x_recv,
    z_send,
    z_recv,
    k_send,
    k_recv,
    m_send,
    m_recv,
    s_send,
    s_recv,
    known,
):
    ny, nx, nt, steps = dims
    g = lax.axis_index("grp")
    t = lax.axis_index("tp")
    y, h = g // nx, g % nx
    span = cache_ref.shape[0]
    group = q_ref.shape[1] // HD // nx
    scale = 1.0 / math.sqrt(HD)

    loads = [
        pltpu.make_async_copy(inc_ref, inc_v, in_sem.at[0]),
        pltpu.make_async_copy(res_ref, res_v, in_sem.at[1]),
        pltpu.make_async_copy(
            proj_ref.at[pl.ds(pl.multiple_of(y * BLK, BLK), BLK), pl.ds(pl.multiple_of(h * 2 * HD, 2 * HD), 2 * HD)],
            proj_v,
            in_sem.at[2],
        ),
        pltpu.make_async_copy(x_ref, xbuf.at[h], in_sem.at[3]),
        pltpu.make_async_copy(q_ref, q_v, in_sem.at[4]),
        pltpu.make_async_copy(idx_hbm, idx_ref, in_sem.at[5]),
        pltpu.make_async_copy(tally_hbm, tally_ref, in_sem.at[6]),
        pltpu.make_async_copy(fill_hbm, fill_ref, in_sem.at[7]),
    ]
    for copy in loads[:4] + loads[5:]:
        copy.start()

    barrier = pltpu.get_barrier_semaphore()
    for k in (1, nt - 1):
        pl.semaphore_signal(barrier, inc=1, device_id=(g, (t + k) % nt), device_id_type=MESH)
    for k in range(1, nx):
        pl.semaphore_signal(barrier, inc=1, device_id=(y * nx + (h + k) % nx, t), device_id_type=MESH)
    for k in range(1, ny):
        pl.semaphore_signal(barrier, inc=1, device_id=(((y + k) % ny) * nx + h, t), device_id_type=MESH)

    loads[4].start()
    cache_loads = []
    for n in range(nx):
        cols = slice(n * 2 * HD, (n + 1) * 2 * HD)
        copy = pltpu.make_async_copy(cache_ref.at[:, cols], cache_v.at[:, cols], cache_sem.at[n])
        copy.start()
        cache_loads.append(copy)

    for copy in loads[:4] + loads[5:]:
        copy.wait()
    first, second, count = idx_ref[0, 0], idx_ref[0, 1], tally_ref[0]
    rows = pl.ds(pl.multiple_of(y * BLK, BLK), BLK)
    for j in range(2):
        keep = ((count > 0) & (first == j)) | ((count > 1) & (second == j))
        summed = inc_v[j] + res_v[j]
        sent = jnp.where(keep, summed.astype(BF16).astype(F32), 0.0)
        err_ref[j] = summed - sent
        cols = slice(j * BLK, (j + 1) * BLK)
        wbuf[rows, cols] = (proj_v[:, cols].astype(F32) + sent).astype(BF16)
    pl.semaphore_wait(barrier, nx + ny)

    reach = [1 << r for r in range(8) if (1 << r) < nt // 2]

    def tell(r):
        for k in (reach[r], nt - reach[r]):
            pl.semaphore_signal(known.at[r], inc=1, device_id=(g, (t + k) % nt), device_id_type=MESH)

    def learn(r):
        if 0 <= r < len(reach):
            pl.semaphore_wait(known.at[r], 2)
            if r + 1 < len(reach):
                tell(r + 1)

    tell(0)

    w_copies = []
    for k in range(1, ny):
        copy = remote(
            wbuf.at[rows], wbuf.at[rows], w_send.at[k], w_recv.at[y], (((y + k) % ny) * nx + h, t)
        )
        copy.start()
        w_copies.append(copy)
    x_copies = []
    for k in range(1, nx):
        copy = remote(xbuf.at[h], xbuf.at[h], x_send.at[k], x_recv.at[h], (y * nx + (h + k) % nx, t))
        copy.start()
        x_copies.append(copy)

    loads[4].wait()
    for n in range(nx * group):
        qf[n * steps : (n + 1) * steps, :] = q_v[:, n * HD : (n + 1) * HD].astype(F32)

    half = group * steps // 2
    position = t * span + lax.broadcasted_iota(jnp.int32, (1, span), 1)
    valid = position < fill_ref[0]
    lane = lax.broadcasted_iota(jnp.int32, (2 * half, HD), 1)
    stats = jnp.zeros((2 * half, HD), F32)
    for copy in cache_loads:
        copy.wait()
    for batch in (range(nx // 2), range(nx // 2, nx)):
        parts = {}
        for n in batch:
            query = qf[n * 2 * half : (n + 1) * 2 * half, :].astype(BF16)
            keys = cache_v[:, n * 2 * HD : n * 2 * HD + HD]
            scores = lax.dot_general(query, keys, (((1,), (1,)), ((), ())), preferred_element_type=F32)
            parts[n] = jnp.where(valid, scores * scale, NEG)
        for n in batch:
            scores = parts[n]
            top = jnp.max(scores, axis=1, keepdims=True)
            probs = jnp.where(valid, jnp.exp(scores - top), 0.0)
            parts[n] = (top, jnp.sum(probs, axis=1, keepdims=True), probs.astype(BF16))
        for n in batch:
            top, total, probs = parts[n]
            values = cache_v[:, n * 2 * HD + HD : (n + 1) * 2 * HD]
            mixed = jnp.dot(probs, values, preferred_element_type=F32).astype(BF16)
            for i in range(2):
                part = slice(i * half, (i + 1) * half)
                msend[2 * n + i] = mixed[part]
                column = jnp.concatenate([top[part], total[part]], axis=0)
                stats = jnp.where(lane == 2 * n + i, column, stats)
        if batch[0] == 0:
            learn(len(reach) - 3)
    learn(len(reach) - 2)
    square = jnp.concatenate([stats, jnp.zeros((HD - 2 * half, HD), F32)], axis=0)
    flipped = square.T
    for n in range(nt):
        ssend[n] = flipped[n : n + 1, :]
    mrecv[t] = msend[t]
    srecv[t] = ssend[t]

    near = reach[-1]

    def send_partials(d, far):
        gap = (d - t + nt) % nt
        close = (gap <= near) | (gap >= nt - near)

        @pl.when((gap > 0) & (close != far))
        def _():
            remote(msend.at[d], mrecv.at[t], m_send, m_recv, (g, d)).start()
            remote(ssend.at[d], srecv.at[t], s_send, s_recv, (g, d)).start()

        return far

    lax.fori_loop(0, nt, send_partials, False)

    for k in range(1, nx):
        o = (h + k) % nx
        remote(xbuf.at[o], xbuf.at[o], x_send.at[k], x_recv.at[o], (g, t)).wait_recv()
    for n in range(nx):
        xf[n * steps : (n + 1) * steps, :] = xbuf[n].astype(F32)
    for k in range(1, ny):
        o = (y + k) % ny
        there = pl.ds(pl.multiple_of(o * BLK, BLK), BLK)
        remote(wbuf.at[there], wbuf.at[there], w_send.at[k], w_recv.at[o], (g, t)).wait_recv()
    product = jnp.dot(xf[...].astype(BF16), wbuf[...], preferred_element_type=F32)
    for n in range(nx):
        zsend[n, :steps, :] = product[n * steps : (n + 1) * steps, :HD]
        zsend[n, steps:, :] = product[n * steps : (n + 1) * steps, HD:]
    zrecv[h] = zsend[h]

    z_copies = []
    for k in range(1, nx):
        o = (h + k) % nx
        copy = remote(zsend.at[o], zrecv.at[h], z_send.at[k], z_recv.at[h], (y * nx + o, t))
        copy.start()
        z_copies.append(copy)

    learn(len(reach) - 1)
    lax.fori_loop(0, nt, send_partials, True)

    def send_sums(i, carry):
        o = i

        @pl.when(o != h)
        def _():
            remote(zsend.at[o], zrecv.at[o], z_send.at[0], z_recv.at[o], (g, t)).wait_recv()

        for j in range(2):
            d = 2 * o + j

            @pl.when(d != t)
            def _():
                remote(zrecv.at[o], kvr.at[t], k_send, k_recv, (g, d)).start()

        return carry

    lax.fori_loop(0, nx, send_sums, 0)
    kvr[t] = zrecv[t // 2]

    others = pl.ds(0, nt - 1)
    m_all = remote(msend.at[others], mrecv.at[others], m_send, m_recv, (g, t))
    s_all_copies = remote(ssend.at[others], srecv.at[others], s_send, s_recv, (g, t))
    k_all = remote(kvr.at[others], kvr.at[others], k_send, k_recv, (g, t))
    m_all.wait_recv()
    s_all_copies.wait_recv()
    for n in range(nt):
        sf[n : n + 1, :] = srecv[n]
    s_all = sf[...]
    peak_all = jnp.max(s_all, axis=0, keepdims=True)
    weight = jnp.exp(s_all - peak_all)
    total_all = jnp.sum(weight * pltpu.roll(s_all, HD - half, 1), axis=0, keepdims=True)
    table = jnp.concatenate(
        [weight, total_all, peak_all, jnp.zeros((HD - nt - 2, HD), F32)], axis=0
    ).T[:half]
    numer = jnp.zeros((half, HD), F32)
    for n in range(nt):
        numer = numer + table[:, n : n + 1] * mrecv[n].astype(F32)
    total = table[:, nt : nt + 1]
    top = table[:, nt + 1 : nt + 2]
    query = qf[pl.ds(pl.multiple_of(t * half, half), half), :]
    step = lax.broadcasted_iota(jnp.int32, (half, 1), 0) % steps

    for copy in w_copies + x_copies + z_copies:
        copy.wait_send()
    m_all.wait_send()
    s_all_copies.wait_send()
    k_all.wait_send()
    k_all.wait_recv()
    fresh = kvr[0]
    for n in range(1, nt):
        fresh = fresh + kvr[n]
    rounded = fresh.astype(BF16).astype(F32)
    kv_ref[...] = jnp.where(t % 2 == 0, rounded[:steps], rounded[steps:]).astype(BF16)
    scores = []
    for u in range(steps):
        s = jnp.sum(query * rounded[u : u + 1, :], axis=1, keepdims=True) * scale
        scores.append(jnp.where(step >= u, s, NEG))
    peak = top
    for s in scores:
        peak = jnp.maximum(peak, s)
    carried = jnp.exp(top - peak)
    denom = total * carried
    numer = numer * carried
    for u in range(steps):
        p = jnp.where(step >= u, jnp.exp(scores[u] - peak), 0.0)
        denom = denom + p
        numer = numer + p * rounded[steps + u : steps + u + 1, :]
    result = numer / denom
    for n in range(half // steps):
        attn_ref[:, n * HD : (n + 1) * HD] = result[n * steps : (n + 1) * steps, :].astype(BF16)


def put_out(err_ref, kv_ref, attn_ref, err_out, kv_out, attn_out, sem):
    copies = [
        pltpu.make_async_copy(err_ref, err_out, sem.at[0]),
        pltpu.make_async_copy(kv_ref, kv_out, sem.at[1]),
        pltpu.make_async_copy(attn_ref, attn_out, sem.at[2]),
    ]
    for copy in copies:
        copy.start()
    for copy in copies:
        copy.wait()


def body(
    trainer_increment,
    trainer_residual,
    partition_tile_indices,
    retained_tallies,
    projection_parameters,
    normalized_activations,
    rotated_questions,
    stored_attention_memory,
    memory_fill_lengths,
):
    local_feats, kvw = projection_parameters.shape
    ny = local_feats // BLK
    nx = kvw // (2 * HD)
    nt = lax.axis_size("tp")
    steps = normalized_activations.shape[0]
    span = stored_attention_memory.shape[1]
    qwidth = rotated_questions.shape[2]
    half = qwidth // HD // nx * steps // 2
    hbm = pl.BlockSpec(memory_space=pltpu.HBM)
    anywhere = pl.BlockSpec(memory_space=pl.ANY)
    vmem = pl.BlockSpec(memory_space=pltpu.VMEM)
    dma = pltpu.SemaphoreType.DMA
    new_error, new_kv, attention = pl.pallas_call(
        functools.partial(kernel, (ny, nx, nt, steps)),
        out_shape=(
            pltpu.VMEM(trainer_increment.shape, F32),
            pltpu.VMEM((steps, kvw // nt), BF16),
            pltpu.VMEM((steps, qwidth // nt), BF16),
        ),
        in_specs=[hbm, hbm, hbm, hbm, hbm, hbm, hbm, hbm, hbm],
        out_specs=(vmem, vmem, vmem),
        scratch_shapes=[
            pltpu.SMEM((1, 2), jnp.int32),
            pltpu.SMEM((1,), jnp.int32),
            pltpu.SMEM((1,), jnp.int32),
            pltpu.VMEM((2, BLK, BLK), F32),
            pltpu.VMEM((2, BLK, BLK), F32),
            pltpu.VMEM((BLK, 2 * HD), BF16),
            pltpu.VMEM((steps, qwidth), BF16),
            pltpu.VMEM((span, kvw), BF16),
            pltpu.VMEM((qwidth // HD * steps, HD), F32),
            pltpu.VMEM((local_feats, 2 * HD), BF16),
            pltpu.VMEM((nx, steps, local_feats), BF16),
            pltpu.VMEM((nx * steps, local_feats), F32),
            pltpu.VMEM((nx, 2 * steps, HD), F32),
            pltpu.VMEM((nx, 2 * steps, HD), F32),
            pltpu.VMEM((nt, 2 * steps, HD), F32),
            pltpu.VMEM((nt, half, HD), BF16),
            pltpu.VMEM((nt, half, HD), BF16),
            pltpu.VMEM((nt, 1, HD), F32),
            pltpu.VMEM((nt, 1, HD), F32),
            pltpu.VMEM((nt, HD), F32),
            dma((8,)),
            dma((nx,)),
            dma((ny,)),
            dma((ny,)),
            dma((nx,)),
            dma((nx,)),
            dma((nx,)),
            dma((nx,)),
            dma,
            dma,
            dma,
            dma,
            dma,
            dma,
            pltpu.SemaphoreType.REGULAR((8,)),
        ],
        compiler_params=pltpu.CompilerParams(collective_id=0, has_side_effects=True),
    )(
        partition_tile_indices,
        retained_tallies,
        memory_fill_lengths,
        trainer_increment,
        trainer_residual,
        projection_parameters,
        normalized_activations.reshape(steps, local_feats),
        rotated_questions.reshape(steps, qwidth),
        stored_attention_memory.reshape(span, kvw),
    )
    outs = (new_error, new_kv, attention)
    new_error, new_kv, attention = pl.pallas_call(
        put_out,
        out_shape=tuple(jax.ShapeDtypeStruct(out.shape, out.dtype) for out in outs),
        in_specs=[anywhere] * 3,
        out_specs=(hbm,) * 3,
        scratch_shapes=[dma((3,))],
    )(*(pltpu.with_memory_space_constraint(out, pltpu.VMEM) for out in outs))
    return (
        new_error,
        new_kv.reshape(steps, 1, kvw // nt),
        attention.reshape(steps, 1, qwidth // nt),
    )


def solution(mesh):
    placed = (
        P(("tp", "grp"), None, None),
        P(("tp", "grp"), None, None),
        P(("tp", "grp"), None),
        P(("tp", "grp")),
        P("tp", None),
        P(None, "grp", "tp"),
        P(None, "grp", None),
        P("grp", "tp", None),
        P("grp"),
    )
    return jax.shard_map(
        body,
        mesh=mesh,
        in_specs=placed,
        out_specs=(P(("tp", "grp"), None, None), P(None, "grp", "tp"), P(None, "grp", "tp")),
        check_vma=False,
    )
```

```python
import functools
import math

import jax
import jax.numpy as jnp
from jax import lax
from jax.experimental import pallas as pl
from jax.experimental.pallas import tpu as pltpu
from jax.sharding import PartitionSpec as P

HD = 128
BLK = 128
NEG = -1e30
F32 = jnp.float32
BF16 = jnp.bfloat16
MESH = pl.DeviceIdType.MESH


def remote(src, dst, send, recv, device):
    return pltpu.make_async_remote_copy(
        src_ref=src, dst_ref=dst, send_sem=send, recv_sem=recv, device_id=device, device_id_type=MESH
    )


def kernel(
    dims,
    idx_hbm,
    tally_hbm,
    fill_hbm,
    inc_ref,
    res_ref,
    proj_ref,
    x_ref,
    q_ref,
    cache_ref,
    err_ref,
    kv_ref,
    attn_ref,
    idx_ref,
    tally_ref,
    fill_ref,
    inc_v,
    res_v,
    proj_v,
    q_v,
    cache_v,
    qf,
    wbuf,
    xbuf,
    xf,
    zsend,
    zrecv,
    kvr,
    msend,
    mrecv,
    ssend,
    srecv,
    sf,
    in_sem,
    cache_sem,
    w_send,
    w_recv,
    x_send,
    x_recv,
    z_send,
    z_recv,
    k_send,
    k_recv,
    m_send,
    m_recv,
    s_send,
    s_recv,
    known,
):
    ny, nx, nt, steps = dims
    g = lax.axis_index("grp")
    t = lax.axis_index("tp")
    y, h = g // nx, g % nx
    span = cache_ref.shape[0]
    group = q_ref.shape[1] // HD // nx
    scale = 1.0 / math.sqrt(HD)

    loads = [
        pltpu.make_async_copy(inc_ref, inc_v, in_sem.at[0]),
        pltpu.make_async_copy(res_ref, res_v, in_sem.at[1]),
        pltpu.make_async_copy(
            proj_ref.at[pl.ds(pl.multiple_of(y * BLK, BLK), BLK), pl.ds(pl.multiple_of(h * 2 * HD, 2 * HD), 2 * HD)],
            proj_v,
            in_sem.at[2],
        ),
        pltpu.make_async_copy(x_ref, xbuf.at[h], in_sem.at[3]),
        pltpu.make_async_copy(q_ref, q_v, in_sem.at[4]),
        pltpu.make_async_copy(idx_hbm, idx_ref, in_sem.at[5]),
        pltpu.make_async_copy(tally_hbm, tally_ref, in_sem.at[6]),
        pltpu.make_async_copy(fill_hbm, fill_ref, in_sem.at[7]),
    ]
    for copy in loads[:4] + loads[5:]:
        copy.start()

    barrier = pltpu.get_barrier_semaphore()
    for k in (1, nt - 1):
        pl.semaphore_signal(barrier, inc=1, device_id=(g, (t + k) % nt), device_id_type=MESH)
    for k in range(1, nx):
        pl.semaphore_signal(barrier, inc=1, device_id=(y * nx + (h + k) % nx, t), device_id_type=MESH)
    for k in range(1, ny):
        pl.semaphore_signal(barrier, inc=1, device_id=(((y + k) % ny) * nx + h, t), device_id_type=MESH)

    loads[4].start()
    cache_loads = []
    for n in range(nx):
        cols = slice(n * 2 * HD, (n + 1) * 2 * HD)
        copy = pltpu.make_async_copy(cache_ref.at[:, cols], cache_v.at[:, cols], cache_sem.at[n])
        copy.start()
        cache_loads.append(copy)

    for copy in loads[:4] + loads[5:]:
        copy.wait()
    first, second, count = idx_ref[0, 0], idx_ref[0, 1], tally_ref[0]
    rows = pl.ds(pl.multiple_of(y * BLK, BLK), BLK)
    for j in range(2):
        keep = ((count > 0) & (first == j)) | ((count > 1) & (second == j))
        summed = inc_v[j] + res_v[j]
        sent = jnp.where(keep, summed.astype(BF16).astype(F32), 0.0)
        err_ref[j] = summed - sent
        cols = slice(j * BLK, (j + 1) * BLK)
        wbuf[rows, cols] = (proj_v[:, cols].astype(F32) + sent).astype(BF16)
    pl.semaphore_wait(barrier, nx + ny)

    reach = [1 << r for r in range(8) if (1 << r) < nt // 2]

    def tell(r):
        for k in (reach[r], nt - reach[r]):
            pl.semaphore_signal(known.at[r], inc=1, device_id=(g, (t + k) % nt), device_id_type=MESH)

    def learn(r):
        if 0 <= r < len(reach):
            pl.semaphore_wait(known.at[r], 2)
            if r + 1 < len(reach):
                tell(r + 1)

    tell(0)

    w_copies = [
        remote(wbuf.at[rows], wbuf.at[rows], w_send.at[k], w_recv.at[y], (((y + k) % ny) * nx + h, t))
        for k in range(1, ny)
    ]

    def send_weights(turn):
        @pl.when(h % 2 == turn)
        def _():
            for copy in w_copies:
                copy.start()

    send_weights(0)
    x_copies = []
    for k in range(1, nx):
        copy = remote(xbuf.at[h], xbuf.at[h], x_send.at[k], x_recv.at[h], (y * nx + (h + k) % nx, t))
        copy.start()
        x_copies.append(copy)

    learn(len(reach) - 3)

    loads[4].wait()
    for n in range(nx * group):
        qf[n * steps : (n + 1) * steps, :] = q_v[:, n * HD : (n + 1) * HD].astype(F32)

    half = group * steps // 2
    position = t * span + lax.broadcasted_iota(jnp.int32, (1, span), 1)
    valid = position < fill_ref[0]
    lane = lax.broadcasted_iota(jnp.int32, (2 * half, HD), 1)
    stats = jnp.zeros((2 * half, HD), F32)
    for copy in cache_loads:
        copy.wait()
    for batch in (range(nx // 2), range(nx // 2, nx)):
        parts = {}
        for n in batch:
            query = qf[n * 2 * half : (n + 1) * 2 * half, :].astype(BF16)
            keys = cache_v[:, n * 2 * HD : n * 2 * HD + HD]
            scores = lax.dot_general(query, keys, (((1,), (1,)), ((), ())), preferred_element_type=F32)
            parts[n] = jnp.where(valid, scores * scale, NEG)
        for n in batch:
            scores = parts[n]
            top = jnp.max(scores, axis=1, keepdims=True)
            probs = jnp.where(valid, jnp.exp(scores - top), 0.0)
            parts[n] = (top, jnp.sum(probs, axis=1, keepdims=True), probs.astype(BF16))
        for n in batch:
            top, total, probs = parts[n]
            values = cache_v[:, n * 2 * HD + HD : (n + 1) * 2 * HD]
            mixed = jnp.dot(probs, values, preferred_element_type=F32).astype(BF16)
            for i in range(2):
                part = slice(i * half, (i + 1) * half)
                msend[2 * n + i] = mixed[part]
                column = jnp.concatenate([top[part], total[part]], axis=0)
                stats = jnp.where(lane == 2 * n + i, column, stats)
        if batch[0] == 0:
            send_weights(1)
            learn(len(reach) - 2)
    square = jnp.concatenate([stats, jnp.zeros((HD - 2 * half, HD), F32)], axis=0)
    flipped = square.T
    for n in range(nt):
        ssend[n] = flipped[n : n + 1, :]
    mrecv[t] = msend[t]
    srecv[t] = ssend[t]

    near = reach[-1]

    def send_partials(d, far):
        gap = (d - t + nt) % nt
        close = (gap <= near) | (gap >= nt - near)

        @pl.when((gap > 0) & (close != far))
        def _():
            remote(msend.at[d], mrecv.at[t], m_send, m_recv, (g, d)).start()
            remote(ssend.at[d], srecv.at[t], s_send, s_recv, (g, d)).start()

        return far

    lax.fori_loop(0, nt, send_partials, False)

    for k in range(1, nx):
        o = (h + k) % nx
        remote(xbuf.at[o], xbuf.at[o], x_send.at[k], x_recv.at[o], (g, t)).wait_recv()
    for n in range(nx):
        xf[n * steps : (n + 1) * steps, :] = xbuf[n].astype(F32)
    for k in range(1, ny):
        o = (y + k) % ny
        there = pl.ds(pl.multiple_of(o * BLK, BLK), BLK)
        remote(wbuf.at[there], wbuf.at[there], w_send.at[k], w_recv.at[o], (g, t)).wait_recv()
    product = jnp.dot(xf[...].astype(BF16), wbuf[...], preferred_element_type=F32)
    for n in range(nx):
        zsend[n, :steps, :] = product[n * steps : (n + 1) * steps, :HD]
        zsend[n, steps:, :] = product[n * steps : (n + 1) * steps, HD:]
    zrecv[h] = zsend[h]

    z_copies = []
    for k in range(1, nx):
        o = (h + k) % nx
        copy = remote(zsend.at[o], zrecv.at[h], z_send.at[k], z_recv.at[h], (y * nx + o, t))
        copy.start()
        z_copies.append(copy)

    learn(len(reach) - 1)
    lax.fori_loop(0, nt, send_partials, True)

    def send_sums(i, carry):
        o = i

        @pl.when(o != h)
        def _():
            remote(zsend.at[o], zrecv.at[o], z_send.at[0], z_recv.at[o], (g, t)).wait_recv()

        for j in range(2):
            d = 2 * o + j

            @pl.when(d != t)
            def _():
                remote(zrecv.at[o], kvr.at[t], k_send, k_recv, (g, d)).start()

        return carry

    lax.fori_loop(0, nx, send_sums, 0)
    kvr[t] = zrecv[t // 2]

    others = pl.ds(0, nt - 1)
    m_all = remote(msend.at[others], mrecv.at[others], m_send, m_recv, (g, t))
    s_all_copies = remote(ssend.at[others], srecv.at[others], s_send, s_recv, (g, t))
    k_all = remote(kvr.at[others], kvr.at[others], k_send, k_recv, (g, t))
    m_all.wait_recv()
    s_all_copies.wait_recv()
    for n in range(nt):
        sf[n : n + 1, :] = srecv[n]
    s_all = sf[...]
    peak_all = jnp.max(s_all, axis=0, keepdims=True)
    weight = jnp.exp(s_all - peak_all)
    total_all = jnp.sum(weight * pltpu.roll(s_all, HD - half, 1), axis=0, keepdims=True)
    table = jnp.concatenate(
        [weight, total_all, peak_all, jnp.zeros((HD - nt - 2, HD), F32)], axis=0
    ).T[:half]
    numer = jnp.zeros((half, HD), F32)
    for n in range(nt):
        numer = numer + table[:, n : n + 1] * mrecv[n].astype(F32)
    total = table[:, nt : nt + 1]
    top = table[:, nt + 1 : nt + 2]
    query = qf[pl.ds(pl.multiple_of(t * half, half), half), :]
    step = lax.broadcasted_iota(jnp.int32, (half, 1), 0) % steps

    for copy in w_copies + x_copies + z_copies:
        copy.wait_send()
    m_all.wait_send()
    s_all_copies.wait_send()
    k_all.wait_send()
    k_all.wait_recv()
    fresh = kvr[0]
    for n in range(1, nt):
        fresh = fresh + kvr[n]
    rounded = fresh.astype(BF16).astype(F32)
    kv_ref[...] = jnp.where(t % 2 == 0, rounded[:steps], rounded[steps:]).astype(BF16)
    scores = []
    for u in range(steps):
        s = jnp.sum(query * rounded[u : u + 1, :], axis=1, keepdims=True) * scale
        scores.append(jnp.where(step >= u, s, NEG))
    peak = top
    for s in scores:
        peak = jnp.maximum(peak, s)
    carried = jnp.exp(top - peak)
    denom = total * carried
    numer = numer * carried
    for u in range(steps):
        p = jnp.where(step >= u, jnp.exp(scores[u] - peak), 0.0)
        denom = denom + p
        numer = numer + p * rounded[steps + u : steps + u + 1, :]
    result = numer / denom
    for n in range(half // steps):
        attn_ref[:, n * HD : (n + 1) * HD] = result[n * steps : (n + 1) * steps, :].astype(BF16)


def put_out(err_ref, kv_ref, attn_ref, err_out, kv_out, attn_out, sem):
    copies = [
        pltpu.make_async_copy(err_ref, err_out, sem.at[0]),
        pltpu.make_async_copy(kv_ref, kv_out, sem.at[1]),
        pltpu.make_async_copy(attn_ref, attn_out, sem.at[2]),
    ]
    for copy in copies:
        copy.start()
    for copy in copies:
        copy.wait()


def body(
    trainer_increment,
    trainer_residual,
    partition_tile_indices,
    retained_tallies,
    projection_parameters,
    normalized_activations,
    rotated_questions,
    stored_attention_memory,
    memory_fill_lengths,
):
    local_feats, kvw = projection_parameters.shape
    ny = local_feats // BLK
    nx = kvw // (2 * HD)
    nt = lax.axis_size("tp")
    steps = normalized_activations.shape[0]
    span = stored_attention_memory.shape[1]
    qwidth = rotated_questions.shape[2]
    half = qwidth // HD // nx * steps // 2
    hbm = pl.BlockSpec(memory_space=pltpu.HBM)
    anywhere = pl.BlockSpec(memory_space=pl.ANY)
    vmem = pl.BlockSpec(memory_space=pltpu.VMEM)
    dma = pltpu.SemaphoreType.DMA
    new_error, new_kv, attention = pl.pallas_call(
        functools.partial(kernel, (ny, nx, nt, steps)),
        out_shape=(
            pltpu.VMEM(trainer_increment.shape, F32),
            pltpu.VMEM((steps, kvw // nt), BF16),
            pltpu.VMEM((steps, qwidth // nt), BF16),
        ),
        in_specs=[hbm, hbm, hbm, hbm, hbm, hbm, hbm, hbm, hbm],
        out_specs=(vmem, vmem, vmem),
        scratch_shapes=[
            pltpu.SMEM((1, 2), jnp.int32),
            pltpu.SMEM((1,), jnp.int32),
            pltpu.SMEM((1,), jnp.int32),
            pltpu.VMEM((2, BLK, BLK), F32),
            pltpu.VMEM((2, BLK, BLK), F32),
            pltpu.VMEM((BLK, 2 * HD), BF16),
            pltpu.VMEM((steps, qwidth), BF16),
            pltpu.VMEM((span, kvw), BF16),
            pltpu.VMEM((qwidth // HD * steps, HD), F32),
            pltpu.VMEM((local_feats, 2 * HD), BF16),
            pltpu.VMEM((nx, steps, local_feats), BF16),
            pltpu.VMEM((nx * steps, local_feats), F32),
            pltpu.VMEM((nx, 2 * steps, HD), F32),
            pltpu.VMEM((nx, 2 * steps, HD), F32),
            pltpu.VMEM((nt, 2 * steps, HD), F32),
            pltpu.VMEM((nt, half, HD), BF16),
            pltpu.VMEM((nt, half, HD), BF16),
            pltpu.VMEM((nt, 1, HD), F32),
            pltpu.VMEM((nt, 1, HD), F32),
            pltpu.VMEM((nt, HD), F32),
            dma((8,)),
            dma((nx,)),
            dma((ny,)),
            dma((ny,)),
            dma((nx,)),
            dma((nx,)),
            dma((nx,)),
            dma((nx,)),
            dma,
            dma,
            dma,
            dma,
            dma,
            dma,
            pltpu.SemaphoreType.REGULAR((8,)),
        ],
        compiler_params=pltpu.CompilerParams(collective_id=0, has_side_effects=True),
    )(
        partition_tile_indices,
        retained_tallies,
        memory_fill_lengths,
        trainer_increment,
        trainer_residual,
        projection_parameters,
        normalized_activations.reshape(steps, local_feats),
        rotated_questions.reshape(steps, qwidth),
        stored_attention_memory.reshape(span, kvw),
    )
    outs = (new_error, new_kv, attention)
    new_error, new_kv, attention = pl.pallas_call(
        put_out,
        out_shape=tuple(jax.ShapeDtypeStruct(out.shape, out.dtype) for out in outs),
        in_specs=[anywhere] * 3,
        out_specs=(hbm,) * 3,
        scratch_shapes=[dma((3,))],
    )(*(pltpu.with_memory_space_constraint(out, pltpu.VMEM) for out in outs))
    return (
        new_error,
        new_kv.reshape(steps, 1, kvw // nt),
        attention.reshape(steps, 1, qwidth // nt),
    )


def solution(mesh):
    placed = (
        P(("tp", "grp"), None, None),
        P(("tp", "grp"), None, None),
        P(("tp", "grp"), None),
        P(("tp", "grp")),
        P("tp", None),
        P(None, "grp", "tp"),
        P(None, "grp", None),
        P("grp", "tp", None),
        P("grp"),
    )
    return jax.shard_map(
        body,
        mesh=mesh,
        in_specs=placed,
        out_specs=(P(("tp", "grp"), None, None), P(None, "grp", "tp"), P(None, "grp", "tp")),
        check_vma=False,
    )
```

```python
import functools
import math

import jax
import jax.numpy as jnp
from jax import lax
from jax.experimental import pallas as pl
from jax.experimental.pallas import tpu as pltpu
from jax.sharding import PartitionSpec as P

HD = 128
BLK = 128
NEG = -1e30
F32 = jnp.float32
BF16 = jnp.bfloat16
MESH = pl.DeviceIdType.MESH


def remote(src, dst, send, recv, device):
    return pltpu.make_async_remote_copy(
        src_ref=src, dst_ref=dst, send_sem=send, recv_sem=recv, device_id=device, device_id_type=MESH
    )


def kernel(
    dims,
    idx_hbm,
    tally_hbm,
    fill_hbm,
    inc_ref,
    res_ref,
    proj_ref,
    x_ref,
    q_ref,
    cache_ref,
    err_ref,
    kv_ref,
    attn_ref,
    idx_ref,
    tally_ref,
    fill_ref,
    inc_v,
    res_v,
    proj_v,
    q_v,
    cache_v,
    qf,
    wbuf,
    xbuf,
    xf,
    zsend,
    zrecv,
    kvr,
    msend,
    mrecv,
    ssend,
    srecv,
    sf,
    in_sem,
    cache_sem,
    w_send,
    w_recv,
    x_send,
    x_recv,
    z_send,
    z_recv,
    k_send,
    k_recv,
    m_send,
    m_recv,
    s_send,
    s_recv,
    known,
):
    ny, nx, nt, steps = dims
    g = lax.axis_index("grp")
    t = lax.axis_index("tp")
    y, h = g // nx, g % nx
    span = cache_ref.shape[0]
    group = q_ref.shape[1] // HD // nx
    scale = 1.0 / math.sqrt(HD)

    loads = [
        pltpu.make_async_copy(inc_ref, inc_v, in_sem.at[0]),
        pltpu.make_async_copy(res_ref, res_v, in_sem.at[1]),
        pltpu.make_async_copy(
            proj_ref.at[pl.ds(pl.multiple_of(y * BLK, BLK), BLK), pl.ds(pl.multiple_of(h * 2 * HD, 2 * HD), 2 * HD)],
            proj_v,
            in_sem.at[2],
        ),
        pltpu.make_async_copy(x_ref, xbuf.at[h], in_sem.at[3]),
        pltpu.make_async_copy(q_ref, q_v, in_sem.at[4]),
        pltpu.make_async_copy(idx_hbm, idx_ref, in_sem.at[5]),
        pltpu.make_async_copy(tally_hbm, tally_ref, in_sem.at[6]),
        pltpu.make_async_copy(fill_hbm, fill_ref, in_sem.at[7]),
    ]
    barrier = pltpu.get_barrier_semaphore()
    for k in (1, nt - 1):
        pl.semaphore_signal(barrier, inc=1, device_id=(g, (t + k) % nt), device_id_type=MESH)
    for k in range(1, nx):
        pl.semaphore_signal(barrier, inc=1, device_id=(y * nx + (h + k) % nx, t), device_id_type=MESH)
    for k in range(1, ny):
        pl.semaphore_signal(barrier, inc=1, device_id=(((y + k) % ny) * nx + h, t), device_id_type=MESH)

    for copy in loads[:4] + loads[5:]:
        copy.start()

    for copy in loads[:4] + loads[5:]:
        copy.wait()
    first, second, count = idx_ref[0, 0], idx_ref[0, 1], tally_ref[0]
    rows = pl.ds(pl.multiple_of(y * BLK, BLK), BLK)
    for j in range(2):
        keep = ((count > 0) & (first == j)) | ((count > 1) & (second == j))
        summed = inc_v[j] + res_v[j]
        sent = jnp.where(keep, summed.astype(BF16).astype(F32), 0.0)
        err_ref[j] = summed - sent
        cols = slice(j * BLK, (j + 1) * BLK)
        wbuf[rows, cols] = (proj_v[:, cols].astype(F32) + sent).astype(BF16)
    pl.semaphore_wait(barrier, nx + ny)

    reach = [1 << r for r in range(8) if (1 << r) < nt // 2]

    def tell(r):
        for k in (reach[r], nt - reach[r]):
            pl.semaphore_signal(known.at[r], inc=1, device_id=(g, (t + k) % nt), device_id_type=MESH)

    def learn(r):
        if 0 <= r < len(reach):
            pl.semaphore_wait(known.at[r], 2)
            if r + 1 < len(reach):
                tell(r + 1)

    tell(0)

    w_copies = [
        remote(wbuf.at[rows], wbuf.at[rows], w_send.at[k], w_recv.at[y], (((y + k) % ny) * nx + h, t))
        for k in range(1, ny)
    ]

    def send_weights(turn):
        @pl.when(h % 2 == turn)
        def _():
            for copy in w_copies:
                copy.start()

    send_weights(0)
    x_copies = []
    for k in range(1, nx):
        copy = remote(xbuf.at[h], xbuf.at[h], x_send.at[k], x_recv.at[h], (y * nx + (h + k) % nx, t))
        copy.start()
        x_copies.append(copy)

    loads[4].start()
    cache_loads = []
    for n in range(nx):
        cols = slice(n * 2 * HD, (n + 1) * 2 * HD)
        copy = pltpu.make_async_copy(cache_ref.at[:, cols], cache_v.at[:, cols], cache_sem.at[n])
        copy.start()
        cache_loads.append(copy)

    learn(len(reach) - 3)

    loads[4].wait()
    for n in range(nx * group):
        qf[n * steps : (n + 1) * steps, :] = q_v[:, n * HD : (n + 1) * HD].astype(F32)

    half = group * steps // 2
    position = t * span + lax.broadcasted_iota(jnp.int32, (1, span), 1)
    valid = position < fill_ref[0]
    lane = lax.broadcasted_iota(jnp.int32, (2 * half, HD), 1)
    stats = jnp.zeros((2 * half, HD), F32)
    for copy in cache_loads:
        copy.wait()
    for batch in (range(nx // 2), range(nx // 2, nx)):
        parts = {}
        for n in batch:
            query = qf[n * 2 * half : (n + 1) * 2 * half, :].astype(BF16)
            keys = cache_v[:, n * 2 * HD : n * 2 * HD + HD]
            scores = lax.dot_general(query, keys, (((1,), (1,)), ((), ())), preferred_element_type=F32)
            parts[n] = jnp.where(valid, scores * scale, NEG)
        for n in batch:
            scores = parts[n]
            top = jnp.max(scores, axis=1, keepdims=True)
            probs = jnp.where(valid, jnp.exp(scores - top), 0.0)
            parts[n] = (top, jnp.sum(probs, axis=1, keepdims=True), probs.astype(BF16))
        for n in batch:
            top, total, probs = parts[n]
            values = cache_v[:, n * 2 * HD + HD : (n + 1) * 2 * HD]
            mixed = jnp.dot(probs, values, preferred_element_type=F32).astype(BF16)
            for i in range(2):
                part = slice(i * half, (i + 1) * half)
                msend[2 * n + i] = mixed[part]
                column = jnp.concatenate([top[part], total[part]], axis=0)
                stats = jnp.where(lane == 2 * n + i, column, stats)
        if batch[0] == 0:
            send_weights(1)
            learn(len(reach) - 2)
    square = jnp.concatenate([stats, jnp.zeros((HD - 2 * half, HD), F32)], axis=0)
    flipped = square.T
    for n in range(nt):
        ssend[n] = flipped[n : n + 1, :]
    mrecv[t] = msend[t]
    srecv[t] = ssend[t]

    near = reach[-1]

    def send_partials(d, far):
        gap = (d - t + nt) % nt
        close = (gap <= near) | (gap >= nt - near)

        @pl.when((gap > 0) & (close != far))
        def _():
            remote(msend.at[d], mrecv.at[t], m_send, m_recv, (g, d)).start()
            remote(ssend.at[d], srecv.at[t], s_send, s_recv, (g, d)).start()

        return far

    lax.fori_loop(0, nt, send_partials, False)

    for k in range(1, nx):
        o = (h + k) % nx
        remote(xbuf.at[o], xbuf.at[o], x_send.at[k], x_recv.at[o], (g, t)).wait_recv()
    for n in range(nx):
        xf[n * steps : (n + 1) * steps, :] = xbuf[n].astype(F32)
    for k in range(1, ny):
        o = (y + k) % ny
        there = pl.ds(pl.multiple_of(o * BLK, BLK), BLK)
        remote(wbuf.at[there], wbuf.at[there], w_send.at[k], w_recv.at[o], (g, t)).wait_recv()
    product = jnp.dot(xf[...].astype(BF16), wbuf[...], preferred_element_type=F32)
    for n in range(nx):
        zsend[n, :steps, :] = product[n * steps : (n + 1) * steps, :HD]
        zsend[n, steps:, :] = product[n * steps : (n + 1) * steps, HD:]
    zrecv[h] = zsend[h]

    z_copies = []
    for k in range(1, nx):
        o = (h + k) % nx
        copy = remote(zsend.at[o], zrecv.at[h], z_send.at[k], z_recv.at[h], (y * nx + o, t))
        copy.start()
        z_copies.append(copy)

    learn(len(reach) - 1)
    lax.fori_loop(0, nt, send_partials, True)

    def send_sums(i, carry):
        o = i

        @pl.when(o != h)
        def _():
            remote(zsend.at[o], zrecv.at[o], z_send.at[0], z_recv.at[o], (g, t)).wait_recv()

        for j in range(2):
            d = 2 * o + j

            @pl.when(d != t)
            def _():
                remote(zrecv.at[o], kvr.at[t], k_send, k_recv, (g, d)).start()

        return carry

    lax.fori_loop(0, nx, send_sums, 0)
    kvr[t] = zrecv[t // 2]

    others = pl.ds(0, nt - 1)
    m_all = remote(msend.at[others], mrecv.at[others], m_send, m_recv, (g, t))
    s_all_copies = remote(ssend.at[others], srecv.at[others], s_send, s_recv, (g, t))
    k_all = remote(kvr.at[others], kvr.at[others], k_send, k_recv, (g, t))
    m_all.wait_recv()
    s_all_copies.wait_recv()
    for n in range(nt):
        sf[n : n + 1, :] = srecv[n]
    s_all = sf[...]
    peak_all = jnp.max(s_all, axis=0, keepdims=True)
    weight = jnp.exp(s_all - peak_all)
    total_all = jnp.sum(weight * pltpu.roll(s_all, HD - half, 1), axis=0, keepdims=True)
    table = jnp.concatenate(
        [weight, total_all, peak_all, jnp.zeros((HD - nt - 2, HD), F32)], axis=0
    ).T[:half]
    numer = jnp.zeros((half, HD), F32)
    for n in range(nt):
        numer = numer + table[:, n : n + 1] * mrecv[n].astype(F32)
    total = table[:, nt : nt + 1]
    top = table[:, nt + 1 : nt + 2]
    query = qf[pl.ds(pl.multiple_of(t * half, half), half), :]
    step = lax.broadcasted_iota(jnp.int32, (half, 1), 0) % steps

    for copy in w_copies + x_copies + z_copies:
        copy.wait_send()
    m_all.wait_send()
    s_all_copies.wait_send()
    k_all.wait_send()
    k_all.wait_recv()
    fresh = kvr[0]
    for n in range(1, nt):
        fresh = fresh + kvr[n]
    rounded = fresh.astype(BF16).astype(F32)
    kv_ref[...] = jnp.where(t % 2 == 0, rounded[:steps], rounded[steps:]).astype(BF16)
    scores = []
    for u in range(steps):
        s = jnp.sum(query * rounded[u : u + 1, :], axis=1, keepdims=True) * scale
        scores.append(jnp.where(step >= u, s, NEG))
    peak = top
    for s in scores:
        peak = jnp.maximum(peak, s)
    carried = jnp.exp(top - peak)
    denom = total * carried
    numer = numer * carried
    for u in range(steps):
        p = jnp.where(step >= u, jnp.exp(scores[u] - peak), 0.0)
        denom = denom + p
        numer = numer + p * rounded[steps + u : steps + u + 1, :]
    result = numer / denom
    for n in range(half // steps):
        attn_ref[:, n * HD : (n + 1) * HD] = result[n * steps : (n + 1) * steps, :].astype(BF16)


def put_out(err_ref, kv_ref, attn_ref, err_out, kv_out, attn_out, sem):
    copies = [
        pltpu.make_async_copy(err_ref, err_out, sem.at[0]),
        pltpu.make_async_copy(kv_ref, kv_out, sem.at[1]),
        pltpu.make_async_copy(attn_ref, attn_out, sem.at[2]),
    ]
    for copy in copies:
        copy.start()
    for copy in copies:
        copy.wait()


def body(
    trainer_increment,
    trainer_residual,
    partition_tile_indices,
    retained_tallies,
    projection_parameters,
    normalized_activations,
    rotated_questions,
    stored_attention_memory,
    memory_fill_lengths,
):
    local_feats, kvw = projection_parameters.shape
    ny = local_feats // BLK
    nx = kvw // (2 * HD)
    nt = lax.axis_size("tp")
    steps = normalized_activations.shape[0]
    span = stored_attention_memory.shape[1]
    qwidth = rotated_questions.shape[2]
    half = qwidth // HD // nx * steps // 2
    hbm = pl.BlockSpec(memory_space=pltpu.HBM)
    anywhere = pl.BlockSpec(memory_space=pl.ANY)
    vmem = pl.BlockSpec(memory_space=pltpu.VMEM)
    dma = pltpu.SemaphoreType.DMA
    new_error, new_kv, attention = pl.pallas_call(
        functools.partial(kernel, (ny, nx, nt, steps)),
        out_shape=(
            pltpu.VMEM(trainer_increment.shape, F32),
            pltpu.VMEM((steps, kvw // nt), BF16),
            pltpu.VMEM((steps, qwidth // nt), BF16),
        ),
        in_specs=[hbm, hbm, hbm, hbm, hbm, hbm, hbm, hbm, hbm],
        out_specs=(vmem, vmem, vmem),
        scratch_shapes=[
            pltpu.SMEM((1, 2), jnp.int32),
            pltpu.SMEM((1,), jnp.int32),
            pltpu.SMEM((1,), jnp.int32),
            pltpu.VMEM((2, BLK, BLK), F32),
            pltpu.VMEM((2, BLK, BLK), F32),
            pltpu.VMEM((BLK, 2 * HD), BF16),
            pltpu.VMEM((steps, qwidth), BF16),
            pltpu.VMEM((span, kvw), BF16),
            pltpu.VMEM((qwidth // HD * steps, HD), F32),
            pltpu.VMEM((local_feats, 2 * HD), BF16),
            pltpu.VMEM((nx, steps, local_feats), BF16),
            pltpu.VMEM((nx * steps, local_feats), F32),
            pltpu.VMEM((nx, 2 * steps, HD), F32),
            pltpu.VMEM((nx, 2 * steps, HD), F32),
            pltpu.VMEM((nt, 2 * steps, HD), F32),
            pltpu.VMEM((nt, half, HD), BF16),
            pltpu.VMEM((nt, half, HD), BF16),
            pltpu.VMEM((nt, 1, HD), F32),
            pltpu.VMEM((nt, 1, HD), F32),
            pltpu.VMEM((nt, HD), F32),
            dma((8,)),
            dma((nx,)),
            dma((ny,)),
            dma((ny,)),
            dma((nx,)),
            dma((nx,)),
            dma((nx,)),
            dma((nx,)),
            dma,
            dma,
            dma,
            dma,
            dma,
            dma,
            pltpu.SemaphoreType.REGULAR((8,)),
        ],
        compiler_params=pltpu.CompilerParams(collective_id=0, has_side_effects=True),
    )(
        partition_tile_indices,
        retained_tallies,
        memory_fill_lengths,
        trainer_increment,
        trainer_residual,
        projection_parameters,
        normalized_activations.reshape(steps, local_feats),
        rotated_questions.reshape(steps, qwidth),
        stored_attention_memory.reshape(span, kvw),
    )
    outs = (new_error, new_kv, attention)
    new_error, new_kv, attention = pl.pallas_call(
        put_out,
        out_shape=tuple(jax.ShapeDtypeStruct(out.shape, out.dtype) for out in outs),
        in_specs=[anywhere] * 3,
        out_specs=(hbm,) * 3,
        scratch_shapes=[dma((3,))],
    )(*(pltpu.with_memory_space_constraint(out, pltpu.VMEM) for out in outs))
    return (
        new_error,
        new_kv.reshape(steps, 1, kvw // nt),
        attention.reshape(steps, 1, qwidth // nt),
    )


def solution(mesh):
    placed = (
        P(("tp", "grp"), None, None),
        P(("tp", "grp"), None, None),
        P(("tp", "grp"), None),
        P(("tp", "grp")),
        P("tp", None),
        P(None, "grp", "tp"),
        P(None, "grp", None),
        P("grp", "tp", None),
        P("grp"),
    )
    return jax.shard_map(
        body,
        mesh=mesh,
        in_specs=placed,
        out_specs=(P(("tp", "grp"), None, None), P(None, "grp", "tp"), P(None, "grp", "tp")),
        check_vma=False,
    )
```
